32 devices in a mesh: group: 2 (over y), sta: 4 (over z), win: 2 (over x), freq: 2 (over core).
Axes of the slice: x: 2, y: 2, z: 4, core: 2. Of those that a mesh axis runs over, the one named last changes fastest.
Arguments:
- records: float32 [1024, 4, 3600], P(('group', 'sta'), 'win', 'freq'), parts along dimension 0, may hold values from -6 to 6
- valid_counts: int32 [8], P(('group', 'sta')), parts along dimension 0, may hold values from 64 to 128, as said below
- pair_blocks: int32 [8, 2], P('group'), parts along dimension 0, may hold values from 0 to 3, as said below
Outputs:
- pair_spectra: bfloat16 [8, 2, 256, 2, 128, 128], P(('group', 'sta'), 'freq', 'win'), parts along dimension 0
The draws below stay inside these ranges and needn't reach their ends.
There are 2 independent parts, one for each index of `group`. The reference program is written for one: setup_inputs(seed, part) draws one part's arguments, and reference() takes and returns one part's arrays. A program takes and returns all parts, laid end to end along the dimension named above; each array names one. Nothing has to cross between parts.
Inputs may be any that keep to these rules, and one draw needn't show every extreme that they name: The stations of block i at positions below valid_counts[i] are live, the others are masked out. `pair_blocks`: slot k belongs to index k // 1 of sta and names two station blocks.
All inputs are finite; a program needn't handle non-finite values.
Results may differ from the reference program's by a relative error of at most 0.001.
Values may be sent and summed in bfloat16 or wider, within the bound.
A program may use at most 64 MiB of HBM per device.

```python
import math
import jax
import jax.numpy as jnp
from jax import lax

BLOCK = 128
SAMPLES = 3600
BINS = 512
HALF_WIDTH = 10
PAIR_DEV = 1
NBLOCKS = 4
STATIONS = 512
WINDOWS = 4
NPAIR = 4
BANDS = 2
BAND = 256


def draw_valid_counts(key, part):
    counts = jax.random.randint(key, (NBLOCKS,), BLOCK // 2, BLOCK + 1)
    full_block = jax.random.randint(jax.random.fold_in(key, 1), (), 0, NBLOCKS)
    counts = counts.at[full_block].set(BLOCK)
    low_block = (full_block + 1 + jax.random.randint(jax.random.fold_in(key, 2), (), 0, NBLOCKS - 1)) % NBLOCKS
    return counts.at[low_block].set(BLOCK // 2).astype(jnp.int32)


def draw_pair_blocks(key, part):
    slot_ids = jnp.arange(NPAIR, dtype=jnp.int32)
    owners = slot_ids // PAIR_DEV
    offset_base = jax.random.randint(jax.random.fold_in(key, 11), (), 0, NBLOCKS - 1)
    reach = 1 + (slot_ids + offset_base) % (NBLOCKS - 1)
    second = (owners + reach) % NBLOCKS
    firsts = jnp.tile(jax.random.permutation(jax.random.fold_in(key, 12), NBLOCKS).astype(jnp.int32), PAIR_DEV)
    return jnp.stack((firsts, second), axis=1).astype(jnp.int32)


def shard_levels(own_key, dims, cuts, least, high):
    level = 1.0
    for axis_at, parts in cuts:
        steps = jax.random.uniform(jax.random.fold_in(jax.random.fold_in(own_key, 6), axis_at), (parts,), jnp.float32, least / len(cuts), high / len(cuts))
        level = level * jnp.repeat(jnp.exp(steps), dims[axis_at] // parts).reshape((-1,) + (1,) * (len(dims) - 1 - axis_at))
    return level


def normal_values(stream_key, extent, deviation, limit, shards=(), kind=jnp.bfloat16):
    gain = shard_levels(stream_key, extent, shards, -0.22, 0.18) if shards else 1.0
    values = jax.random.normal(stream_key, extent, jnp.float32) * deviation * gain
    return jnp.minimum(jnp.maximum(values, -limit), limit).astype(kind)


def setup_inputs(seed: int = 0, part: int = 0) -> dict:
    arg_keys = jax.random.split(jax.random.key(seed), 4)
    own_keys = jax.random.split(jax.random.fold_in(arg_keys[3], part), 4)
    return {
        "records": normal_values(own_keys[0], (STATIONS, WINDOWS, SAMPLES), 1.0, 6.0, ((0, 4), (1, 2), (2, 2)), jnp.float32),
        "valid_counts": draw_valid_counts(jax.random.fold_in(jax.random.fold_in(arg_keys[3], part), 71), part),
        "pair_blocks": draw_pair_blocks(jax.random.fold_in(jax.random.fold_in(arg_keys[3], part), 71), part),
    }


TWO_PI = 2.0 * math.pi
AMP_FLOOR = 0.1
PRECISE = lax.Precision.HIGHEST

def taper_of(sample_index, length_all):
    edge_len = length_all // 20
    position = jnp.minimum(sample_index, length_all - 1 - sample_index)
    ramped = 0.5 * (1.0 - jnp.cos(math.pi * (position.astype(jnp.float32) + 0.5) / edge_len))
    return jnp.where(position < edge_len, ramped, 1.0)

def dft_tables(bin_start, amount, sample_start, sample_count, length_all):
    bin_index = bin_start + 1 + lax.broadcasted_iota(jnp.int32, (amount, sample_count), 0)
    sample_index = sample_start + lax.broadcasted_iota(jnp.int32, (amount, sample_count), 1)
    angles = (bin_index * sample_index % length_all).astype(jnp.float32) * (TWO_PI / length_all)
    weight = taper_of(sample_index, length_all) / math.sqrt(length_all)
    return (jnp.cos(angles) * weight, -jnp.sin(angles) * weight)

def whiten_block(block_records, live_count):
    cos_table, sin_table = dft_tables(0, BINS, 0, SAMPLES, SAMPLES)
    real_part = jnp.einsum('kn,swn->kws', cos_table, block_records, precision=PRECISE)
    imag_part = jnp.einsum('kn,swn->kws', sin_table, block_records, precision=PRECISE)
    live_mask = (jnp.arange(BLOCK, dtype=jnp.int32) < live_count).astype(jnp.float32)
    spectrum = jnp.stack((real_part, imag_part), 2) * live_mask
    magnitude = jnp.sqrt(spectrum[:, :, 0] * spectrum[:, :, 0] + spectrum[:, :, 1] * spectrum[:, :, 1])
    padded = jnp.pad(magnitude, ((HALF_WIDTH, HALF_WIDTH), (0, 0), (0, 0)))
    summed = padded[0:BINS]
    for lag_step in range(1, 2 * HALF_WIDTH + 1):
        summed = summed + padded[lag_step:lag_step + BINS]
    global_bin = jnp.arange(BINS, dtype=jnp.int32)
    counted = (jnp.minimum(global_bin + HALF_WIDTH, BINS - 1) - jnp.maximum(global_bin - HALF_WIDTH, 0) + 1).astype(jnp.float32)
    smooth = summed / counted[:, None, None]
    return spectrum / jnp.maximum(smooth, AMP_FLOOR)[:, :, None, :]

def cross_pair(left_block, right_block):
    left_real = left_block[:, :, 0]
    left_imag = left_block[:, :, 1]
    stacked = jnp.stack((jnp.stack((left_real, left_imag), 2), jnp.stack((left_imag, -left_real), 2)), 1)
    factor = 1.0 / math.sqrt(left_block.shape[1])
    return jnp.einsum('fpwqa,fwqb->fpab', stacked, right_block, precision=PRECISE) * factor

def reference(records, valid_counts, pair_blocks):
    grouped = records.reshape(NBLOCKS, BLOCK, WINDOWS, SAMPLES)

    def whiten_item(item_pair):
        return whiten_block(item_pair[0], item_pair[1])
    spectra = lax.map(whiten_item, (grouped, valid_counts))

    def one_pair(pair_row):
        left_block = spectra[pair_row[0]]
        right_block = spectra[pair_row[1]]
        return cross_pair(left_block, right_block).astype(jnp.bfloat16)
    result = lax.map(one_pair, pair_blocks)
    return result.reshape(NPAIR, BANDS, BAND, 2, BLOCK, BLOCK)
```

```python
import functools
import math

import jax
import jax.numpy as jnp
import numpy as np
from jax import lax
from jax.experimental import pallas as pl
from jax.experimental.pallas import tpu as pltpu
from jax.sharding import PartitionSpec as P

SAMPLES = 3600
BINS = 512
HALF_WIDTH = 10
AMP_FLOOR = 0.1
HALO = 16
BAND = BINS // 2
SIDE = (BAND + HALO) // 2
ROWS = 2 * SIDE
FOLD = 912
TILE = 8
LEVEL_ROWS = 8
LEVELS = 32766.0
MESH = pl.DeviceIdType.MESH


def band_bins(band, parity):
    own = np.arange(BAND // 2) * 2 + band * BAND
    halo = np.arange(HALO // 2) * 2 + (BAND if band == 0 else BAND - HALO)
    return np.concatenate([own, halo]) + parity


def dft_table():
    half = SAMPLES // 2
    table = np.zeros((2, 2, 2, ROWS, FOLD), jnp.bfloat16)
    at = np.arange(half // 2 + 1)
    weight = np.where(at == half // 2, 0.5, 1.0) / math.sqrt(SAMPLES)
    for band in range(2):
        angles = []
        for parity in range(2):
            phase = (band_bins(band, parity)[:, None] + 1) * at[None] % SAMPLES
            angles.append(phase * (2.0 * math.pi / SAMPLES))
        summed = np.concatenate([np.cos(angles[1]), -np.sin(angles[0])]) * weight
        differed = np.concatenate([np.cos(angles[0]), -np.sin(angles[1])]) * weight
        for stream, value in enumerate((summed, differed)):
            high = value.astype(jnp.bfloat16)
            low = value - high.astype(np.float64)
            table[band, stream, 0, :, :at.size] = high
            table[band, stream, 1, :, :at.size] = low.astype(jnp.bfloat16)
    return table


def split(value):
    high = value.astype(jnp.bfloat16)
    return high, (value - high.astype(jnp.float32)).astype(jnp.bfloat16)


def dot(a, b):
    return jnp.dot(a, b, preferred_element_type=jnp.float32)


def chunking(wins):
    side = BAND // wins // 2
    chunks = min(4, side // TILE)
    return chunks, side // chunks


def chunk_rows(chunk, wins, local_wins):
    return 2 * chunking(wins)[1] * local_wins + (LEVEL_ROWS if chunk == 0 else 0)


def pair_masks(windows, lanes):
    half = windows * TILE
    depth = 2 * half
    row_bin = lax.broadcasted_iota(jnp.int32, (depth, 2 * lanes), 0) % TILE
    col_odd = lax.broadcasted_iota(jnp.int32, (depth, 2 * lanes), 1) // lanes
    keep = row_bin % 2 == col_odd
    lane_pair = lax.broadcasted_iota(jnp.int32, (lanes, 2 * depth), 1) % TILE // 2
    return keep, lane_pair


def turned(value):
    high = value.astype(jnp.bfloat16).astype(jnp.float32)
    both = jnp.concatenate([high, value - high], axis=0)
    return both.T.astype(jnp.bfloat16)


def pair_group(left, right, masks, store):
    keep, lane_pair = masks
    lanes = left[0].shape[1]
    streams = (
        turned(jnp.concatenate([left[0], left[1]], axis=0)),
        turned(jnp.concatenate([left[1], -left[0]], axis=0)),
    )
    held = jnp.concatenate([right[0], right[1]], axis=0)
    held = jnp.where(keep, jnp.concatenate([held, held], axis=1), 0.0)
    high, low = split(held)
    held = jnp.concatenate([high, high, low, low], axis=0)
    for m in range(TILE // 2):
        for p in range(2):
            part = jnp.where(lane_pair == m, streams[p], jnp.zeros_like(streams[p]))
            part = jnp.concatenate([part, part], axis=1)
            out = dot(part, held).astype(jnp.bfloat16)
            store(2 * m, p, out[:, :lanes])
            store(2 * m + 1, p, out[:, lanes:])


def unpacked(words, levels):
    re = [(word >> 16).astype(jnp.float32) * level for word, level in zip(words, levels)]
    im = [((word << 16) >> 16).astype(jnp.float32) * level for word, level in zip(words, levels)]
    return jnp.concatenate(re, axis=0), jnp.concatenate(im, axis=0)


def spread_levels(rows, scale):
    return [
        jnp.broadcast_to(jnp.exp2(row.astype(jnp.float32) * 0.25) * scale, (TILE, row.shape[1]))
        for row in rows
    ]


def spectra_kernel(stas, wins, local_wins, fused, *refs):
    chunks, side = chunking(wins)
    live_ref, slots_ref, x_ref, table_ref, prod_ref, last_ref, level_ref, *refs = refs
    blocks, refs = refs[:chunks], refs[chunks:]
    codes, refs = refs[:chunks], refs[chunks:]
    staged, refs = refs[:chunks], refs[chunks:]
    (
        tab, raw, fold, give, got, own, white,
        tab_sem, raw_sem, fs_sem, fr_sem, ws_sem, wr_sem, rs_sem, rr_sem, ls_sem, lr_sem,
    ) = refs
    sta = lax.axis_index("sta")
    win = lax.axis_index("win")
    freq = lax.axis_index("freq")
    other = 1 - freq
    samples, lanes = x_ref.shape[1:]
    windows = wins * local_wins
    sub = BAND // wins
    last = stas - 1
    has_right = sta < last
    has_left = sta > 0

    def raw_copy(w):
        return pltpu.make_async_copy(x_ref.at[w], raw.at[w], raw_sem.at[w])

    def table_copy(step):
        band = other if step < 2 else freq
        return pltpu.make_async_copy(table_ref.at[band, step % 2], tab.at[step], tab_sem.at[step])

    for w in range(local_wins):
        raw_copy(w).start()
    for step in range(4):
        table_copy(step).start()

    barrier = pltpu.get_barrier_semaphore()
    pl.semaphore_signal(barrier, inc=1, device_id={"freq": other}, device_id_type=MESH)
    for hop in range(1, wins):
        pl.semaphore_signal(
            barrier, inc=1, device_id={"win": lax.rem(win + hop, wins)}, device_id_type=MESH
        )

    @pl.when(has_right)
    def _():
        pl.semaphore_signal(barrier, inc=1, device_id={"sta": sta + 1}, device_id_type=MESH)

    @pl.when(has_left)
    def _():
        pl.semaphore_signal(barrier, inc=1, device_id={"sta": sta - 1}, device_id_type=MESH)

    edge = SAMPLES // 20
    span = -(-edge // 8) * 8
    begin = pl.multiple_of(freq * (samples - span), 8)
    at = begin + lax.broadcasted_iota(jnp.int32, (span, lanes), 0)
    position = jnp.where(freq == 0, at, samples - 1 - at)
    ramp = 0.5 * (1.0 - jnp.cos(math.pi * (position.astype(jnp.float32) + 0.5) / edge))
    ramp = jnp.where(position < edge, ramp, 1.0)
    sub_row = lax.broadcasted_iota(jnp.int32, (TILE, lanes), 0)
    mirror = lax.rem(TILE - sub_row, TILE)
    tiles = samples // TILE

    def mirrored(w, tile):
        value = raw[w, pl.ds(pl.multiple_of(tile * TILE, TILE), TILE), :]
        return jnp.take_along_axis(value, mirror, axis=0, mode="promise_in_bounds")

    for w in range(local_wins):
        part = slice(w * lanes, (w + 1) * lanes)
        raw_copy(w).wait()
        raw[w, pl.ds(begin, span), :] = raw[w, pl.ds(begin, span), :] * ramp

        def folding(step, before, w=w, part=part):
            for inner in range(3):
                sums, differences = [], []
                for k in range(2):
                    tile = (step * 3 + inner) * 2 + k
                    after = mirrored(w, tiles - 1 - tile)
                    back = jnp.where(sub_row == 0, before, after)
                    ahead = raw[w, pl.ds(pl.multiple_of(tile * TILE, TILE), TILE), :]
                    sums.append(ahead + back)
                    differences.append(ahead - back)
                    before = after
                at = pl.ds(pl.multiple_of((step * 3 + inner) * 2 * TILE, 2 * TILE), 2 * TILE)
                for stream, value in enumerate((sums, differences)):
                    high, low = split(jnp.concatenate(value, axis=0))
                    fold[stream, 0, at, part] = high
                    fold[stream, 1, at, part] = low
            return before

        lax.fori_loop(0, FOLD // (6 * TILE), folding, jnp.zeros((TILE, lanes), jnp.float32))

    flip = jnp.where(freq == 1, -1.0, 1.0).astype(jnp.float32)
    row = lax.broadcasted_iota(jnp.int32, (ROWS, 1), 0)
    signs = (jnp.where(row < SIDE, 1.0, flip), jnp.where(row < SIDE, flip, 1.0))

    def partial(step):
        stream = step % 2
        table_copy(step).wait()
        value = dot(tab[step, 0], fold[stream, 0]) + (
            dot(tab[step, 0], fold[stream, 1]) + dot(tab[step, 1], fold[stream, 0])
        )
        return value * signs[stream]

    def freq_copy(step):
        return pltpu.make_async_remote_copy(
            src_ref=give.at[step], dst_ref=got.at[step],
            send_sem=fs_sem.at[step], recv_sem=fr_sem.at[step],
            device_id={"freq": other}, device_id_type=MESH,
        )

    give[0] = partial(0)
    ends = jnp.where(has_right, 1, 0) + jnp.where(has_left, 1, 0)
    pl.semaphore_wait(barrier, wins + ends)
    freq_copy(0).start()
    give[1] = partial(1)
    freq_copy(1).start()
    for step in range(2):
        own[step] = partial(2 + step)
    for step in range(2):
        freq_copy(step).wait_recv()

    summed_part = own[0] + got[0]
    differed_part = own[1] + got[1]
    real = jnp.concatenate([differed_part[:SIDE], summed_part[:SIDE]], axis=0)
    imag = jnp.concatenate([summed_part[SIDE:], differed_part[SIDE:]], axis=0)
    magnitude = jnp.sqrt(real * real + imag * imag)
    row = lax.broadcasted_iota(jnp.int32, (BAND, ROWS), 0)
    col = lax.broadcasted_iota(jnp.int32, (BAND, ROWS), 1)
    half = BAND // 2
    row = jnp.where(row < half, 2 * row, 2 * (row - half) + 1)
    odd = jnp.where(col < SIDE, 0, 1)
    at = col - odd * SIDE
    place = 2 * at + odd - jnp.where((at >= half) & (freq == 1), BAND + HALO, 0)
    box = ((place - row <= HALF_WIDTH) & (row - place <= HALF_WIDTH)).astype(jnp.float32)
    box = box.astype(jnp.bfloat16)
    high, low = split(magnitude)
    summed = dot(box, high) + dot(box, low)
    bin_row = lax.broadcasted_iota(jnp.int32, (BAND, 1), 0)
    bin_at = freq * BAND + jnp.where(bin_row < half, 2 * bin_row, 2 * (bin_row - half) + 1)
    counted = (
        jnp.minimum(bin_at + HALF_WIDTH, BINS - 1) - jnp.maximum(bin_at - HALF_WIDTH, 0) + 1
    ).astype(jnp.float32)
    station = lax.broadcasted_iota(jnp.int32, (1, local_wins * lanes), 1) % lanes
    live = (station < live_ref[0]).astype(jnp.float32)
    inverse = live / jnp.maximum(summed / counted, AMP_FLOOR)
    for parity in range(2):
        rows = slice(parity * SIDE, parity * SIDE + half)
        scale = inverse[parity * half:(parity + 1) * half]
        white[0, parity] = real[rows] * scale
        white[1, parity] = imag[rows] * scale

    def encode(hop, slots):
        dest = lax.rem(win + hop, wins)
        for w in range(local_wins):
            part = slice(w * lanes, (w + 1) * lanes)
            rows = pl.ds(pl.multiple_of(dest * (sub // 2), TILE), sub // 2)
            values = [[white[v, parity, rows, part] for parity in range(2)] for v in range(2)]
            peak = functools.reduce(jnp.maximum, [jnp.abs(v) for pair in values for v in pair])
            peak = jnp.max(peak, axis=0, keepdims=True)
            level = jnp.ceil(jnp.log2(jnp.maximum(peak, 1e-30)) * 4.0 + 0.01)
            factor = jnp.exp2(level * -0.25) * LEVELS
            slots[0][w:w + 1, :] = level.astype(jnp.int32)
            for c in range(chunks):
                base = LEVEL_ROWS if c == 0 else 0
                for parity in range(2):
                    for t in range(side // TILE):
                        rows = slice(c * side + t * TILE, c * side + (t + 1) * TILE)
                        top = jnp.round(values[0][parity][rows] * factor).astype(jnp.int32)
                        low = jnp.round(values[1][parity][rows] * factor).astype(jnp.int32)
                        to = base + ((parity * (side // TILE) + t) * local_wins + w) * TILE
                        slots[c][to:to + TILE, :] = top * 65536 + (low & 65535)

    def win_copy(c, hop):
        return pltpu.make_async_remote_copy(
            src_ref=codes[c].at[hop - 1], dst_ref=blocks[c].at[sta, win],
            send_sem=ws_sem.at[c, hop], recv_sem=wr_sem.at[c, hop],
            device_id={"win": lax.rem(win + hop, wins)}, device_id_type=MESH,
        )

    def picks(end, toward):
        mine = [jnp.abs(toward - slots_ref[end, k]) for k in range(2)]
        none_far, none_near = jnp.int32(-1), jnp.int32(stas)
        far = functools.reduce(jnp.maximum, [jnp.where(b < last, b, none_far) for b in mine])
        near = functools.reduce(jnp.minimum, [jnp.where(b < last, b, none_near) for b in mine])
        return jnp.clip(far, 1, last - 1), jnp.clip(near, 0, last - 2)

    right_picks = picks(last, 0)
    left_picks = picks(0, last)

    def source(j):
        return lax.rem(win - j + wins, wins)

    def hop_copy(c, j, t, right, src, index):
        send, recv = (rs_sem, rr_sem) if right else (ls_sem, lr_sem)
        return pltpu.make_async_remote_copy(
            src_ref=src, dst_ref=blocks[c].at[index, source(j)],
            send_sem=send.at[c, j, t], recv_sem=recv.at[c, j, t],
            device_id={"sta": sta + 1 if right else sta - 1}, device_id_type=MESH,
        )

    def whole_copy(c, j, t, right):
        index = sta - t if right else sta + t
        return hop_copy(c, j, t, right, blocks[c].at[index, source(j)], index)

    def pick_copy(c, j, which, right):
        far = last - 1 if which == 0 else 0
        index = far if right else last - far
        src = staged[c].at[0 if right else 1, which, j]
        return hop_copy(c, j, which, right, src, index)

    def arrived(c, j, t, right):
        inner = (sta >= t) & (sta < last) if right else (last - sta >= t) & (sta > 0)

        @pl.when(inner)
        def _():
            index = sta - t if right else sta + t
            hop_copy(c, j, t - 1, right, blocks[c].at[index, source(j)], index).wait_recv()

    def pick(c, j, which, right):
        def at(b):
            return blocks[c][b if right else last - b, source(j)]

        chosen = (right_picks if right else left_picks)[which]
        first, count = (1, last - 1) if which == 0 else (0, last - 1)
        value = at(first)
        for b in range(first + 1, first + count):
            value = jnp.where(chosen == b, at(b), value)
        staged[c][0 if right else 1, which, j] = value
        pick_copy(c, j, which, right).start()

    def event(c, j, t):
        for right in (True, False):
            if not (isinstance(t, int) and t == 0):
                arrived(c, j, t, right)
            behind = sta if right else last - sta

            @pl.when((behind >= t) & (behind < last - 1))
            def _(right=right):
                whole_copy(c, j, t, right).start()

            for which in range(2):
                due = last - 2 + which
                if not isinstance(t, int) or t == due:
                    @pl.when((behind == last - 1) & (t == due))
                    def _(right=right, which=which):
                        pick(c, j, which, right)

    def ended(c, j):
        for right in (True, False):
            @pl.when((sta == last) if right else (sta == 0))
            def _(right=right):
                for which in range(2):
                    pick_copy(c, j, which, right).wait_recv()

    def drain(c, j):
        for right in (True, False):
            behind = sta if right else last - sta
            for t in range(last - 1):
                @pl.when((behind >= t) & (behind < last - 1))
                def _(right=right, t=t):
                    whole_copy(c, j, t, right).wait_send()

            @pl.when(behind == last - 1)
            def _(right=right):
                for which in range(2):
                    pick_copy(c, j, which, right).wait_send()

    encode(0, [blocks[c].at[sta, win] for c in range(chunks)])
    for c in range(chunks):
        event(c, 0, 0)
    for hop in range(1, wins):
        encode(hop, [codes[c].at[hop - 1] for c in range(chunks)])
        for c in range(chunks):
            win_copy(c, hop).start()

    def lies(b):
        at_last = jnp.where(b == last, last, jnp.where(b == right_picks[0], last - 1, 0))
        far = last - left_picks[0]
        at_first = jnp.where(b == 0, 0, jnp.where(b == far, 1, last))
        return jnp.where(sta == last, at_last, jnp.where(sta == 0, at_first, b))

    left_at = lies(slots_ref[sta, 0])
    right_at = lies(slots_ref[sta, 1])
    order = [(s, w) for s in range(wins) for w in range(local_wins)]

    def products(c, levels, masks):
        base = LEVEL_ROWS if c == 0 else 0
        for parity in range(2):
            for t in range(side // TILE):
                parts = []
                for at, level in zip((left_at, right_at), levels):
                    rows = [
                        base + ((parity * (side // TILE) + t) * local_wins + w) * TILE
                        for _, w in order
                    ]
                    words = [
                        blocks[c][at, s, r:r + TILE, :] for (s, _), r in zip(order, rows)
                    ]
                    parts.append(unpacked(words, level))
                first = 2 * (c * side + t * TILE) + parity

                def store(b, p, value, first=first):
                    prod_ref[first + 2 * b, p] = value

                pair_group(*parts, masks, store)

    for c in range(chunks):
        for j in range(1, wins):
            win_copy(c, j).wait_recv()
            event(c, j, 0)
        event(c, 0, 1)
    for t in range(1, last - 1):
        for c in range(chunks):
            for j in range(1, wins):
                event(c, j, t)
            event(c, 0, t + 1)
    masks = pair_masks(windows, lanes)
    levels = None
    for c in range(chunks):
        for j in range(1, wins):
            event(c, j, last - 1)
        for j in range(wins):
            ended(c, j)
        if c == 0:
            levels = []
            for k, at in enumerate((left_at, right_at)):
                scale = (1.0 / math.sqrt(windows) if k else 1.0) / LEVELS
                for s in range(wins):
                    level_ref[k, s] = blocks[0][at, s, :LEVEL_ROWS, :]
                rows = [blocks[0][at, s, w:w + 1, :] for s, w in order]
                levels.append(spread_levels(rows, scale))
        if c < fused:
            products(c, levels, masks)
        else:
            base = LEVEL_ROWS if c == 0 else 0
            for k, at in enumerate((left_at, right_at)):
                for s in range(wins):
                    last_ref[c - fused, k, s] = blocks[c][at, s, base:, :]

    for c in range(chunks):
        for j in range(wins):
            drain(c, j)
        for hop in range(1, wins):
            win_copy(c, hop).wait_send()
    for step in range(2):
        freq_copy(step).wait_send()


def gathered(live, slots, x, table, fused):
    stas = lax.axis_size("sta")
    wins = lax.axis_size("win")
    local_wins, samples, lanes = x.shape
    cols = local_wins * lanes
    chunks, side = chunking(wins)
    dma = pltpu.SemaphoreType.DMA
    smem = pl.BlockSpec(memory_space=pltpu.SMEM)
    hold = pl.BlockSpec(memory_space=pltpu.HBM)
    vmem = pl.BlockSpec(memory_space=pltpu.VMEM)
    rows = [chunk_rows(c, wins, local_wins) for c in range(chunks)]
    near = [2 * side * local_wins] * chunks
    return pl.pallas_call(
        functools.partial(spectra_kernel, stas, wins, local_wins, fused),
        out_shape=(
            jax.ShapeDtypeStruct((fused * 2 * side, 2, lanes, lanes), jnp.bfloat16),
            jax.ShapeDtypeStruct((chunks - fused, 2, wins, near[0], lanes), jnp.int32),
            jax.ShapeDtypeStruct((2, wins, LEVEL_ROWS, lanes), jnp.int32),
        ),
        in_specs=[smem, smem, hold, hold],
        out_specs=(vmem, vmem, vmem),
        scratch_shapes=[
            *[pltpu.VMEM((stas, wins, r, lanes), jnp.int32) for r in rows],
            *[pltpu.VMEM((max(1, wins - 1), r, lanes), jnp.int32) for r in rows],
            *[pltpu.VMEM((2, 2, wins, r, lanes), jnp.int32) for r in rows],
            pltpu.VMEM((4, 2, ROWS, FOLD), jnp.bfloat16),
            pltpu.VMEM((local_wins, samples, lanes), jnp.float32),
            pltpu.VMEM((2, 2, FOLD, cols), jnp.bfloat16),
            pltpu.VMEM((2, ROWS, cols), jnp.float32),
            pltpu.VMEM((2, ROWS, cols), jnp.float32),
            pltpu.VMEM((2, ROWS, cols), jnp.float32),
            pltpu.VMEM((2, 2, BAND // 2, cols), jnp.float32),
            dma((4,)), dma((local_wins,)), dma((2,)), dma((2,)),
            dma((chunks, wins)), dma((chunks, wins)),
            dma((chunks, wins, stas)), dma((chunks, wins, stas)),
            dma((chunks, wins, stas)), dma((chunks, wins, stas)),
        ],
        compiler_params=pltpu.CompilerParams(
            collective_id=0, has_side_effects=True, vmem_limit_bytes=40 << 20
        ),
        name="spectra",
    )(live, slots, *(pltpu.with_memory_space_constraint(v, pltpu.HBM) for v in (x, table)))


def finish_kernel(wins, local_wins, fused, prod_ref, last_ref, level_ref, out_ref, work, prod_sem, work_sem):
    chunks, side = chunking(wins)
    windows = wins * local_wins
    lanes = prod_ref.shape[-1]
    bins = 2 * side
    order = [(s, w) for s in range(wins) for w in range(local_wins)]

    def prod_copy(c):
        at = pl.ds(c * bins, bins)
        return pltpu.make_async_copy(prod_ref.at[at], out_ref.at[at], prod_sem.at[c])

    def work_copy(k):
        at = pl.ds(k * 2 * TILE, 2 * TILE)
        to = pl.ds(fused * bins + k * 2 * TILE, 2 * TILE)
        return pltpu.make_async_copy(work.at[at], out_ref.at[to], work_sem.at[k])

    for c in range(fused):
        prod_copy(c).start()
    masks = pair_masks(windows, lanes)
    levels = [
        spread_levels(
            [level_ref[k, s, w:w + 1, :] for s, w in order],
            (1.0 / math.sqrt(windows) if k else 1.0) / LEVELS,
        )
        for k in range(2)
    ]
    steps = side // TILE
    for c in range(chunks - fused):
        for t in range(steps):
            for parity in range(2):
                parts = []
                for k in range(2):
                    rows = [((parity * steps + t) * local_wins + w) * TILE for _, w in order]
                    words = [last_ref[c, k, s, r:r + TILE, :] for (s, _), r in zip(order, rows)]
                    parts.append(unpacked(words, levels[k]))
                first = 2 * (c * side + t * TILE) + parity

                def store(b, p, value, first=first):
                    work[first + 2 * b, p] = value

                pair_group(*parts, masks, store)
            work_copy(c * steps + t).start()
    for c in range(fused):
        prod_copy(c).wait()
    for k in range((chunks - fused) * steps):
        work_copy(k).wait()


def finished(prod, rest, levels, fused, bins):
    left, _, wins, rows, lanes = rest.shape
    local_wins = rows // (2 * chunking(wins)[1])
    steps = left * (chunking(wins)[1] // TILE)
    vmem = pl.BlockSpec(memory_space=pltpu.VMEM)
    dma = pltpu.SemaphoreType.DMA
    return pl.pallas_call(
        functools.partial(finish_kernel, wins, local_wins, fused),
        out_shape=jax.ShapeDtypeStruct((bins, 2, lanes, lanes), jnp.bfloat16),
        in_specs=[vmem, vmem, vmem],
        out_specs=pl.BlockSpec(memory_space=pltpu.HBM),
        scratch_shapes=[
            pltpu.VMEM((steps * 2 * TILE, 2, lanes, lanes), jnp.bfloat16),
            dma((fused,)), dma((steps,)),
        ],
        compiler_params=pltpu.CompilerParams(vmem_limit_bytes=16 << 20),
        name="finish",
    )(prod, rest, levels)


def local(table, records, valid_counts, pair_blocks):
    wins = lax.axis_size("win")
    chunks, _ = chunking(wins)
    fused = chunks - 1
    x = jnp.transpose(records, (1, 2, 0))
    prod, rest, levels = gathered(valid_counts, pair_blocks, x, jnp.asarray(table), fused)
    return finished(prod, rest, levels, fused, BAND // wins)[None, None]


def solution(mesh):
    in_specs = (P(("group", "sta"), "win", "freq"), P(("group", "sta")), P("group", None))
    out_specs = P(("group", "sta"), "freq", "win", None, None, None)
    body = functools.partial(local, dft_table())
    return jax.shard_map(body, mesh=mesh, in_specs=in_specs, out_specs=out_specs, check_vma=False)
```

```python
import functools
import math

import jax
import jax.numpy as jnp
import numpy as np
from jax import lax
from jax.experimental import pallas as pl
from jax.experimental.pallas import tpu as pltpu
from jax.sharding import PartitionSpec as P

SAMPLES = 3600
BINS = 512
HALF_WIDTH = 10
AMP_FLOOR = 0.1
HALO = 8
BAND = BINS // 2
FOLD = 912
WIDE = 1024
TILE = 8
AHEAD = 2
LEVEL_ROWS = 8
LEVELS = 32766.0
MESH = pl.DeviceIdType.MESH


def part_rows(wins):
    return BAND // wins // 2 + 2 * HALO


def dft_table(wins):
    half = SAMPLES // 2
    rows = part_rows(wins)
    table = np.zeros((2, wins, 2, 4 * rows, WIDE), jnp.bfloat16)
    at = np.arange(half // 2 + 1)
    weight = np.where(at == half // 2, 0.5, 1.0) / math.sqrt(SAMPLES)
    for band in range(2):
        for part in range(wins):
            first = band * BAND + part * (BAND // wins) - 2 * HALO
            waves = []
            for parity in range(2):
                bins = first + 2 * np.arange(rows)[:, None] + parity
                angle = (bins + 1) * at[None] % SAMPLES * (2.0 * math.pi / SAMPLES)
                inside = (bins >= 0) & (bins < BINS)
                waves.append([np.cos(angle) * inside * weight, -np.sin(angle) * inside * weight])
            summed = np.concatenate([waves[1][0], waves[0][1]])
            differed = np.concatenate([waves[0][0], waves[1][1]])
            for stream, value in enumerate((summed, differed)):
                high = value.astype(jnp.bfloat16)
                low = value - high.astype(np.float64)
                table[band, part, stream, :2 * rows, :at.size] = high
                table[band, part, stream, 2 * rows:, :at.size] = low.astype(jnp.bfloat16)
    return table


def split(value):
    high = value.astype(jnp.bfloat16)
    return high, (value - high.astype(jnp.float32)).astype(jnp.bfloat16)


def dot(a, b):
    return jnp.dot(a, b, preferred_element_type=jnp.float32)


def chunking(wins):
    tiles = BAND // wins // 2 // TILE
    counts = [tiles // 4] * 4 if tiles % 4 == 0 else [tiles - tiles // 2, tiles // 2]
    return [(sum(counts[:k]), count) for k, count in enumerate(counts)]


def chunk_rows(chunk, wins, local_wins):
    rows = 2 * chunking(wins)[chunk][1] * TILE * local_wins
    return rows + (LEVEL_ROWS if chunk == 0 else 0)


def pair_masks(windows, lanes):
    half = windows * TILE
    depth = 2 * half
    row_bin = lax.broadcasted_iota(jnp.int32, (depth, 2 * lanes), 0) % TILE
    col_odd = lax.broadcasted_iota(jnp.int32, (depth, 2 * lanes), 1) // lanes
    keep = row_bin % 2 == col_odd
    lane_pair = lax.broadcasted_iota(jnp.int32, (lanes, 2 * depth), 1) % TILE // 2
    return keep, lane_pair


def turned(value):
    high = value.astype(jnp.bfloat16).astype(jnp.float32)
    both = jnp.concatenate([high, value - high], axis=0)
    return both.T.astype(jnp.bfloat16)


def pair_group(left, right, masks, store):
    keep, lane_pair = masks
    lanes = left[0].shape[1]
    streams = (
        turned(jnp.concatenate([left[0], left[1]], axis=0)),
        turned(jnp.concatenate([left[1], -left[0]], axis=0)),
    )
    held = jnp.concatenate([right[0], right[1]], axis=0)
    held = jnp.where(keep, jnp.concatenate([held, held], axis=1), 0.0)
    high, low = split(held)
    held = jnp.concatenate([high, high, low, low], axis=0)
    for m in range(TILE // 2):
        for p in range(2):
            part = jnp.where(lane_pair == m, streams[p], jnp.zeros_like(streams[p]))
            part = jnp.concatenate([part, part], axis=1)
            out = dot(part, held).astype(jnp.bfloat16)
            store(2 * m, p, out[:, :lanes])
            store(2 * m + 1, p, out[:, lanes:])


def unpacked(words, levels):
    re = [(word >> 16).astype(jnp.float32) * level for word, level in zip(words, levels)]
    im = [((word << 16) >> 16).astype(jnp.float32) * level for word, level in zip(words, levels)]
    return jnp.concatenate(re, axis=0), jnp.concatenate(im, axis=0)


def spread_levels(rows, scale):
    return [
        jnp.broadcast_to(jnp.exp2(row.astype(jnp.float32) * 0.25) * scale, (TILE, row.shape[1]))
        for row in rows
    ]


def spectra_kernel(stas, wins, local_wins, fused, *refs):
    parts = chunking(wins)
    chunks = len(parts)
    live_ref, pairs_ref, x_ref, table_ref, prod_ref, last_ref, level_ref, *refs = refs
    blocks, refs = refs[:chunks], refs[chunks:]
    codes, refs = refs[:chunks], refs[chunks:]
    staged, refs = refs[:chunks], refs[chunks:]
    (
        tab, raw, fold, give, got, slots_ref,
        slots_sem, tab_sem, raw_sem, fs_sem, fr_sem, ws_sem, wr_sem, rs_sem, rr_sem, ls_sem, lr_sem,
    ) = refs
    sta = lax.axis_index("sta")
    win = lax.axis_index("win")
    freq = lax.axis_index("freq")
    other = 1 - freq
    samples, lanes = x_ref.shape[1:]
    windows = wins * local_wins
    sub = BAND // wins
    last = stas - 1

    def raw_copy(w):
        return pltpu.make_async_copy(x_ref.at[w], raw.at[w], raw_sem.at[w])

    side_rows = part_rows(wins)
    rows = 2 * side_rows
    reach = last - 1 if stas <= 4 else 1

    def table_copy(hop, mine):
        part = lax.rem(win + hop, wins)
        at = hop * 2 + mine
        return pltpu.make_async_copy(
            table_ref.at[freq if mine else other, part], tab.at[at], tab_sem.at[at]
        )

    slots_copy = pltpu.make_async_copy(pairs_ref, slots_ref, slots_sem)
    for w in range(local_wins):
        raw_copy(w).start()
    for hop in range(wins):
        for mine in range(2):
            table_copy(hop, mine).start()
    slots_copy.start()

    barrier = pltpu.get_barrier_semaphore()
    pl.semaphore_signal(barrier, inc=1, device_id={"freq": other}, device_id_type=MESH)
    greeted = jnp.int32(1)
    for away in range(-reach, reach + 1):
        there = (sta + away >= 0) & (sta + away < stas)
        for hop in range(wins):
            if (away == 0) == (hop == 0):
                continue
            greeted += jnp.where(there, 1, 0)

            @pl.when(there)
            def _(away=away, hop=hop):
                to = {"sta": sta + away, "win": lax.rem(win + hop, wins)}
                pl.semaphore_signal(barrier, inc=1, device_id=to, device_id_type=MESH)

    edge = SAMPLES // 20
    span = -(-edge // 8) * 8
    begin = pl.multiple_of(freq * (samples - span), 8)
    at = begin + lax.broadcasted_iota(jnp.int32, (span, lanes), 0)
    position = jnp.where(freq == 0, at, samples - 1 - at)
    ramp = 0.5 * (1.0 - jnp.cos(math.pi * (position.astype(jnp.float32) + 0.5) / edge))
    ramp = jnp.where(position < edge, ramp, 1.0)
    sub_row = lax.broadcasted_iota(jnp.int32, (TILE, lanes), 0)
    mirror = lax.rem(TILE - sub_row, TILE)
    tiles = samples // TILE

    def mirrored(w, tile):
        value = raw[w, pl.ds(pl.multiple_of(tile * TILE, TILE), TILE), :]
        return jnp.take_along_axis(value, mirror, axis=0, mode="promise_in_bounds")

    for w in range(local_wins):
        part = slice(w * lanes, (w + 1) * lanes)
        raw_copy(w).wait()
        raw[w, pl.ds(begin, span), :] = raw[w, pl.ds(begin, span), :] * ramp

        def folding(step, before, w=w, part=part):
            for inner in range(3):
                sums, differences = [], []
                for k in range(2):
                    tile = (step * 3 + inner) * 2 + k
                    after = mirrored(w, tiles - 1 - tile)
                    back = jnp.where(sub_row == 0, before, after)
                    ahead = raw[w, pl.ds(pl.multiple_of(tile * TILE, TILE), TILE), :]
                    sums.append(ahead + back)
                    differences.append(ahead - back)
                    before = after
                at = pl.ds(pl.multiple_of((step * 3 + inner) * 2 * TILE, 2 * TILE), 2 * TILE)
                for stream, value in enumerate((sums, differences)):
                    high, low = split(jnp.concatenate(value, axis=0))
                    fold[stream, 0, at, part] = high
                    fold[stream, 1, at, part] = low
            return before

        lax.fori_loop(0, FOLD // (6 * TILE), folding, jnp.zeros((TILE, lanes), jnp.float32))

    flip = jnp.where(freq == 1, -1.0, 1.0).astype(jnp.float32)
    row = lax.broadcasted_iota(jnp.int32, (rows, 1), 0)
    signs = (jnp.where(row < side_rows, 1.0, flip), jnp.where(row < side_rows, flip, 1.0))

    count = sub // 2
    row = lax.broadcasted_iota(jnp.int32, (sub, rows), 0)
    col = lax.broadcasted_iota(jnp.int32, (sub, rows), 1)
    row = jnp.where(row < count, 2 * row, 2 * (row - count) + 1) + 2 * HALO
    col = jnp.where(col < side_rows, 2 * col, 2 * (col - side_rows) + 1)
    box = ((col - row <= HALF_WIDTH) & (row - col <= HALF_WIDTH)).astype(jnp.float32)
    box = box.astype(jnp.bfloat16)
    bin_row = lax.broadcasted_iota(jnp.int32, (sub, 1), 0)
    bin_row = jnp.where(bin_row < count, 2 * bin_row, 2 * (bin_row - count) + 1)
    station = lax.broadcasted_iota(jnp.int32, (1, local_wins * lanes), 1) % lanes
    live = (station < live_ref[0]).astype(jnp.float32)

    def partial(hop, step):
        stream = step % 2
        if stream == 0:
            table_copy(hop, step // 2).wait()
        at = hop * 2 + step // 2
        both = dot(tab[at, stream, :, :FOLD], fold[stream, 0])
        value = both[:rows] + (both[rows:] + dot(tab[at, stream, :rows, :FOLD], fold[stream, 1]))
        return value * signs[stream]

    def freq_copy(hop, step):
        return pltpu.make_async_remote_copy(
            src_ref=give.at[hop, step], dst_ref=got.at[hop, step],
            send_sem=fs_sem.at[hop, step], recv_sem=fr_sem.at[hop, step],
            device_id={"freq": other}, device_id_type=MESH,
        )

    def send_partials(hop):
        for step in range(2):
            give[hop, step] = partial(hop, step)
            if hop == 0 and step == 0:
                pl.semaphore_wait(barrier, greeted)
            freq_copy(hop, step).start()

    def encode(hop, own, slots):
        dest = lax.rem(win + hop, wins)
        for step in range(2):
            freq_copy(hop, step).wait_recv()
        summed_part = own[0] + got[hop, 0]
        differed_part = own[1] + got[hop, 1]
        real = (differed_part[:side_rows], summed_part[:side_rows])
        imag = (summed_part[side_rows:], differed_part[side_rows:])
        magnitude = jnp.concatenate([jnp.sqrt(a * a + b * b) for a, b in zip(real, imag)], axis=0)
        high, low = split(magnitude)
        summed = dot(box, high) + dot(box, low)
        bin_at = freq * BAND + dest * sub + bin_row
        counted = (
            jnp.minimum(bin_at + HALF_WIDTH, BINS - 1) - jnp.maximum(bin_at - HALF_WIDTH, 0) + 1
        ).astype(jnp.float32)
        inverse = live / jnp.maximum(summed / counted, AMP_FLOOR)
        inner = slice(HALO, HALO + count)
        white = [
            [v[parity][inner] * inverse[parity * count:(parity + 1) * count] for parity in range(2)]
            for v in (real, imag)
        ]
        for w in range(local_wins):
            part = slice(w * lanes, (w + 1) * lanes)
            values = [[v[:, part] for v in pair] for pair in white]
            peak = functools.reduce(jnp.maximum, [jnp.abs(v) for pair in values for v in pair])
            peak = jnp.max(peak, axis=0, keepdims=True)
            level = jnp.ceil(jnp.log2(jnp.maximum(peak, 1e-30)) * 4.0 + 0.01)
            factor = jnp.exp2(level * -0.25) * LEVELS
            slots[0][w:w + 1, :] = level.astype(jnp.int32)
            for c, (first, tiles) in enumerate(parts):
                base = LEVEL_ROWS if c == 0 else 0
                for parity in range(2):
                    for t in range(tiles):
                        at = slice((first + t) * TILE, (first + t + 1) * TILE)
                        top = jnp.round(values[0][parity][at] * factor).astype(jnp.int32)
                        low = jnp.round(values[1][parity][at] * factor).astype(jnp.int32)
                        to = base + ((parity * tiles + t) * local_wins + w) * TILE
                        slots[c][to:to + TILE, :] = top * 65536 + (low & 65535)

    def win_copy(c, hop):
        return pltpu.make_async_remote_copy(
            src_ref=codes[c].at[hop - 1], dst_ref=blocks[c].at[sta, win],
            send_sem=ws_sem.at[c, hop - 1], recv_sem=wr_sem.at[c, hop - 1],
            device_id={"win": lax.rem(win + hop, wins)}, device_id_type=MESH,
        )

    def slots_of(hop):
        return [blocks[c].at[sta, win] if hop == 0 else codes[c].at[hop - 1] for c in range(chunks)]

    def leave(hop):
        for c in range(chunks):
            if hop:
                win_copy(c, hop).start()
            if hop == 0 and (reach == 1 or c < 2):
                depart(c, hop)

    def picks(end, toward):
        mine = [jnp.abs(toward - slots_ref[k, end]) for k in range(2)]
        none_far, none_near = jnp.int32(-1), jnp.int32(stas)
        far = functools.reduce(jnp.maximum, [jnp.where(b < last, b, none_far) for b in mine])
        near = functools.reduce(jnp.minimum, [jnp.where(b < last, b, none_near) for b in mine])
        return jnp.clip(far, 1, last - 1), jnp.clip(near, 0, last - 2)

    slots_copy.wait()
    right_picks = picks(last, 0)
    left_picks = picks(0, last)

    def source(j):
        return lax.rem(win - j + wins, wins)

    def hop_copy(c, j, t, right, src, to, away=1):
        send, recv = (rs_sem, rr_sem) if right else (ls_sem, lr_sem)
        return pltpu.make_async_remote_copy(
            src_ref=src, dst_ref=blocks[c].at[to[0], to[1]],
            send_sem=send.at[c, j, t], recv_sem=recv.at[c, j, t],
            device_id={"sta": sta + away if right else sta - away}, device_id_type=MESH,
        )

    def own_copy(c, j, t, right):
        to = (sta, source(j))
        return hop_copy(c, j, t, right, blocks[c].at[to[0], to[1]], to, t + 1)

    def relay_copy(c, j, t, right):
        to = (sta - t if right else sta + t, source(j))
        return hop_copy(c, j, t, right, blocks[c].at[to[0], to[1]], to)

    def whole_copy(c, j, t, right):
        return own_copy(c, j, t, right) if reach > 1 or t == 0 else relay_copy(c, j, t, right)

    def sends_whole(t, right):
        behind = sta if right else last - sta
        if reach == 1:
            return (behind >= t) & (behind < last - 1)
        return behind + t + 1 < last

    def pick_copy(c, j, which, right):
        far = last - 1 if which == 0 else 0
        index = far if right else last - far
        src = staged[c].at[0 if right else 1, which, j]
        return hop_copy(c, j, which, right, src, (index, source(j)))

    def arrived(c, j, t, right):
        inner = (sta >= t) & (sta < last) if right else (last - sta >= t) & (sta > 0)

        @pl.when(inner)
        def _():
            to = (sta - t if right else sta + t, source(j))
            hop_copy(c, j, t - 1, right, blocks[c].at[to[0], to[1]], to).wait_recv()

    def pick(c, j, which, right):
        def at(b):
            return blocks[c][b if right else last - b, source(j)]

        chosen = (right_picks if right else left_picks)[which]
        first, count = (1, last - 1) if which == 0 else (0, last - 1)
        value = at(first)
        for b in range(first + 1, first + count):
            value = jnp.where(chosen == b, at(b), value)
        staged[c][0 if right else 1, which, j] = value
        pick_copy(c, j, which, right).start()

    def depart(c, j):
        if j:
            win_copy(c, j).wait_recv()
        for k in range(reach - 1, -1, -1):
            for right in (True, False):
                @pl.when(sends_whole(k, right))
                def _(right=right, k=k):
                    own_copy(c, j, k, right).start()

    def departed(c, j):
        for k in range(reach):
            for right in (True, False):
                @pl.when(sends_whole(k, right))
                def _(right=right, k=k):
                    own_copy(c, j, k, right).wait_send()

    def event(c, j, t):
        for right in (True, False):
            behind = sta if right else last - sta
            arrived(c, j, t, right)
            if reach == 1:
                @pl.when(sends_whole(t, right))
                def _(right=right):
                    relay_copy(c, j, t, right).start()

            for which in range(2):
                if t == last - 2 + which:
                    @pl.when(behind == last - 1)
                    def _(right=right, which=which):
                        pick(c, j, which, right)

    def ended(c, j):
        for right in (True, False):
            @pl.when((sta == last) if right else (sta == 0))
            def _(right=right):
                for which in range(2):
                    pick_copy(c, j, which, right).wait_recv()

    def drain(c, j):
        for right in (True, False):
            behind = sta if right else last - sta
            for t in range(last - 1) if reach == 1 else []:
                @pl.when(sends_whole(t, right))
                def _(right=right, t=t):
                    whole_copy(c, j, t, right).wait_send()

            @pl.when(behind == last - 1)
            def _(right=right):
                for which in range(2):
                    pick_copy(c, j, which, right).wait_send()

    send_partials(0)
    own = [partial(0, step) for step in range(2, 4)]
    for hop in range(1, wins):
        send_partials(hop)
        encode(hop - 1, own, slots_of(hop - 1))
        leave(hop - 1)
        own = [partial(hop, step) for step in range(2, 4)]
    encode(wins - 1, own, slots_of(wins - 1))
    leave(wins - 1)

    def lies(b):
        at_last = jnp.where(b == last, last, jnp.where(b == right_picks[0], last - 1, 0))
        far = last - left_picks[0]
        at_first = jnp.where(b == 0, 0, jnp.where(b == far, 1, last))
        return jnp.where(sta == last, at_last, jnp.where(sta == 0, at_first, b))

    left_at = lies(slots_ref[0, sta])
    right_at = lies(slots_ref[1, sta])
    order = [(s, w) for s in range(wins) for w in range(local_wins)]

    def products(c, levels, masks):
        base = LEVEL_ROWS if c == 0 else 0
        start, tiles = parts[c]
        for parity in range(2):
            for t in range(tiles):
                sides = []
                for at, level in zip((left_at, right_at), levels):
                    rows = [
                        base + ((parity * tiles + t) * local_wins + w) * TILE for _, w in order
                    ]
                    words = [blocks[c][at, s, r:r + TILE, :] for (s, _), r in zip(order, rows)]
                    sides.append(unpacked(words, level))
                first = 2 * (start + t) * TILE + parity

                def store(b, p, value, first=first):
                    prod_ref[first + 2 * b, p] = value

                pair_group(*sides, masks, store)

    def arrivals(c, part, hops):
        for t in hops:
            for j in [0] if part == 0 else range(1, wins):
                event(c, j, t)

    masks = pair_masks(windows, lanes)
    levels = []

    def finish(c):
        for j in range(wins):
            ended(c, j)
        base = LEVEL_ROWS if c == 0 else 0
        for k, at in enumerate((left_at, right_at)):
            if c == 0:
                scale = (1.0 / math.sqrt(windows) if k else 1.0) / LEVELS
                for s in range(wins):
                    level_ref[k, s] = blocks[0][at, s, :LEVEL_ROWS, :]
                rows = [blocks[0][at, s, w:w + 1, :] for s, w in order]
                levels.append(spread_levels(rows, scale))
            if c == fused:
                for s in range(wins):
                    last_ref[k, s] = blocks[c][at, s, base:, :]
        if c < fused:
            products(c, levels, masks)

    hops = range(1, last)
    if reach == 1:
        for c in range(chunks):
            for j in range(1, wins):
                depart(c, j)
        for t in hops[:-1]:
            for c in range(chunks):
                for part in range(2):
                    arrivals(c, part, [t])
        for c in range(chunks):
            for part in range(2):
                arrivals(c, part, hops[-1:])
            finish(c)
    else:
        items = [(c, part) for part in range(2) for c in range(chunks)]
        pending = list(range(chunks))
        for k, (c, part) in enumerate(items):
            for ahead, ahead_part in items[k + AHEAD:k + AHEAD + 1] if k else items[2:1 + AHEAD]:
                for j in [0] if ahead_part == 0 else range(1, wins):
                    depart(ahead, j)
            for j in [0] if part == 0 else range(1, wins):
                departed(c, j)
            arrivals(c, part, hops)
            if part and c >= chunks - 2:
                finish(pending.pop(0))
        for c in pending:
            finish(c)

    for c in range(chunks):
        for j in range(wins):
            drain(c, j)
        for hop in range(1, wins):
            win_copy(c, hop).wait_send()
    for hop in range(wins):
        for step in range(2):
            freq_copy(hop, step).wait_send()


def gathered(live, slots, x, table, fused):
    stas = lax.axis_size("sta")
    wins = lax.axis_size("win")
    local_wins, samples, lanes = x.shape
    cols = local_wins * lanes
    parts = chunking(wins)
    chunks = len(parts)
    dma = pltpu.SemaphoreType.DMA
    smem = pl.BlockSpec(memory_space=pltpu.SMEM)
    hold = pl.BlockSpec(memory_space=pltpu.HBM)
    vmem = pl.BlockSpec(memory_space=pltpu.VMEM)
    rows = [chunk_rows(c, wins, local_wins) for c in range(chunks)]
    rows_in = 2 * part_rows(wins)
    return pl.pallas_call(
        functools.partial(spectra_kernel, stas, wins, local_wins, fused),
        out_shape=(
            jax.ShapeDtypeStruct((2 * parts[fused][0] * TILE, 2, lanes, lanes), jnp.bfloat16),
            jax.ShapeDtypeStruct((2, wins, rows[fused], lanes), jnp.int32),
            jax.ShapeDtypeStruct((2, wins, LEVEL_ROWS, lanes), jnp.int32),
        ),
        in_specs=[smem, hold, hold, hold],
        out_specs=(vmem, vmem, vmem),
        scratch_shapes=[
            *[pltpu.VMEM((stas, wins, r, lanes), jnp.int32) for r in rows],
            *[pltpu.VMEM((max(1, wins - 1), r, lanes), jnp.int32) for r in rows],
            *[pltpu.VMEM((2, 2, wins, r, lanes), jnp.int32) for r in rows],
            pltpu.VMEM((2 * wins, 2, 2 * rows_in, WIDE), jnp.bfloat16),
            pltpu.VMEM((local_wins, samples, lanes), jnp.float32),
            pltpu.VMEM((2, 2, FOLD, cols), jnp.bfloat16),
            pltpu.VMEM((wins, 2, rows_in, cols), jnp.float32),
            pltpu.VMEM((wins, 2, rows_in, cols), jnp.float32),
            pltpu.SMEM((2, stas), jnp.int32),
            dma(()), dma((2 * wins,)), dma((local_wins,)), dma((wins, 2)), dma((wins, 2)),
            dma((chunks, max(1, wins - 1))), dma((chunks, max(1, wins - 1))),
            *[dma((chunks, wins, max(2, stas - 2)))] * 4,
        ],
        compiler_params=pltpu.CompilerParams(
            collective_id=0, has_side_effects=True, vmem_limit_bytes=40 << 20
        ),
        name="spectra",
    )(live, *(pltpu.with_memory_space_constraint(v, pltpu.HBM) for v in (slots, x, table)))


def finish_kernel(wins, local_wins, fused, prod_ref, last_ref, level_ref, out_ref, work, prod_sem, work_sem):
    start, tiles = chunking(wins)[fused]
    windows = wins * local_wins
    lanes = prod_ref.shape[-1]
    order = [(s, w) for s in range(wins) for w in range(local_wins)]
    shares = prod_sem.shape[0]
    share = prod_ref.shape[0] // shares

    def prod_copy(k):
        at = pl.ds(k * share, share)
        return pltpu.make_async_copy(prod_ref.at[at], out_ref.at[at], prod_sem.at[k])

    def work_copy(t):
        at = pl.ds(t * 2 * TILE, 2 * TILE)
        to = pl.ds((start + t) * 2 * TILE, 2 * TILE)
        return pltpu.make_async_copy(work.at[at], out_ref.at[to], work_sem.at[t])

    for k in range(shares):
        prod_copy(k).start()
    masks = pair_masks(windows, lanes)
    levels = [
        spread_levels(
            [level_ref[k, s, w:w + 1, :] for s, w in order],
            (1.0 / math.sqrt(windows) if k else 1.0) / LEVELS,
        )
        for k in range(2)
    ]
    for t in range(tiles):
        for parity in range(2):
            sides = []
            for k in range(2):
                rows = [((parity * tiles + t) * local_wins + w) * TILE for _, w in order]
                words = [last_ref[k, s, r:r + TILE, :] for (s, _), r in zip(order, rows)]
                sides.append(unpacked(words, levels[k]))
            first = 2 * t * TILE + parity

            def store(b, p, value, first=first):
                work[first + 2 * b, p] = value

            pair_group(*sides, masks, store)
        work_copy(t).start()
    for k in range(shares):
        prod_copy(k).wait()
    for t in range(tiles):
        work_copy(t).wait()


def finished(prod, rest, levels, fused, bins, local_wins):
    wins, lanes = rest.shape[1], rest.shape[-1]
    tiles = chunking(wins)[fused][1]
    shares = math.gcd(4, prod.shape[0])
    vmem = pl.BlockSpec(memory_space=pltpu.VMEM)
    dma = pltpu.SemaphoreType.DMA
    return pl.pallas_call(
        functools.partial(finish_kernel, wins, local_wins, fused),
        out_shape=jax.ShapeDtypeStruct((bins, 2, lanes, lanes), jnp.bfloat16),
        in_specs=[vmem, vmem, vmem],
        out_specs=pl.BlockSpec(memory_space=pltpu.HBM),
        scratch_shapes=[
            pltpu.VMEM((tiles * 2 * TILE, 2, lanes, lanes), jnp.bfloat16),
            dma((shares,)), dma((tiles,)),
        ],
        compiler_params=pltpu.CompilerParams(vmem_limit_bytes=16 << 20),
        name="finish",
    )(prod, rest, levels)


def local(table, records, valid_counts, pair_blocks):
    wins = lax.axis_size("win")
    fused = len(chunking(wins)) - 1
    x = jnp.transpose(records, (1, 2, 0))
    prod, rest, levels = gathered(valid_counts, pair_blocks.T, x, jnp.asarray(table), fused)
    return finished(prod, rest, levels, fused, BAND // wins, records.shape[1])[None, None]


def solution(mesh):
    in_specs = (P(("group", "sta"), "win", "freq"), P(("group", "sta")), P("group", None))
    out_specs = P(("group", "sta"), "freq", "win", None, None, None)
    body = functools.partial(local, dft_table(mesh.shape["win"]))
    return jax.shard_map(body, mesh=mesh, in_specs=in_specs, out_specs=out_specs, check_vma=False)
```

```python
import functools
import math

import jax
import jax.numpy as jnp
import numpy as np
from jax import lax
from jax.experimental import pallas as pl
from jax.experimental.pallas import tpu as pltpu
from jax.sharding import PartitionSpec as P

SAMPLES = 3600
BINS = 512
HALF_WIDTH = 10
AMP_FLOOR = 0.1
HALO = 8
BAND = BINS // 2
FOLD = 912
WIDE = 1024
TILE = 8
AHEAD = 2
LEVEL_ROWS = 8
LEVELS = 32766.0
MESH = pl.DeviceIdType.MESH


def part_rows(wins):
    return BAND // wins // 2 + 2 * HALO


def dft_table(wins):
    half = SAMPLES // 2
    rows = part_rows(wins)
    table = np.zeros((2, wins, 2, 4 * rows, WIDE), jnp.bfloat16)
    at = np.arange(half // 2 + 1)
    weight = np.where(at == half // 2, 0.5, 1.0) / math.sqrt(SAMPLES)
    for band in range(2):
        for part in range(wins):
            first = band * BAND + part * (BAND // wins) - 2 * HALO
            waves = []
            for parity in range(2):
                bins = first + 2 * np.arange(rows)[:, None] + parity
                angle = (bins + 1) * at[None] % SAMPLES * (2.0 * math.pi / SAMPLES)
                inside = (bins >= 0) & (bins < BINS)
                waves.append([np.cos(angle) * inside * weight, -np.sin(angle) * inside * weight])
            summed = np.concatenate([waves[1][0], waves[0][1]])
            differed = np.concatenate([waves[0][0], waves[1][1]])
            for stream, value in enumerate((summed, differed)):
                high = value.astype(jnp.bfloat16)
                low = value - high.astype(np.float64)
                table[band, part, stream, :2 * rows, :at.size] = high
                table[band, part, stream, 2 * rows:, :at.size] = low.astype(jnp.bfloat16)
    return table


def split(value):
    high = value.astype(jnp.bfloat16)
    return high, (value - high.astype(jnp.float32)).astype(jnp.bfloat16)


def dot(a, b):
    return jnp.dot(a, b, preferred_element_type=jnp.float32)


def chunking(wins):
    tiles = BAND // wins // 2 // TILE
    counts = [tiles // 4] * 4 if tiles % 4 == 0 else [tiles - tiles // 2, tiles // 2]
    return [(sum(counts[:k]), count) for k, count in enumerate(counts)]


def chunk_rows(chunk, wins, local_wins):
    rows = 2 * chunking(wins)[chunk][1] * TILE * local_wins
    return rows + (LEVEL_ROWS if chunk == 0 else 0)


def pair_masks(windows, lanes):
    half = windows * TILE
    depth = 2 * half
    row_bin = lax.broadcasted_iota(jnp.int32, (depth, 2 * lanes), 0) % TILE
    col_odd = lax.broadcasted_iota(jnp.int32, (depth, 2 * lanes), 1) // lanes
    keep = row_bin % 2 == col_odd
    lane_pair = lax.broadcasted_iota(jnp.int32, (lanes, 2 * depth), 1) % TILE // 2
    return keep, lane_pair


def turned(value):
    high = value.astype(jnp.bfloat16).astype(jnp.float32)
    both = jnp.concatenate([high, value - high], axis=0)
    return both.T.astype(jnp.bfloat16)


def pair_group(left, right, masks, store):
    keep, lane_pair = masks
    lanes = left[0].shape[1]
    streams = (
        turned(jnp.concatenate([left[0], left[1]], axis=0)),
        turned(jnp.concatenate([left[1], -left[0]], axis=0)),
    )
    held = jnp.concatenate([right[0], right[1]], axis=0)
    held = jnp.where(keep, jnp.concatenate([held, held], axis=1), 0.0)
    high, low = split(held)
    held = jnp.concatenate([high, high, low, low], axis=0)
    for m in range(TILE // 2):
        for p in range(2):
            part = jnp.where(lane_pair == m, streams[p], jnp.zeros_like(streams[p]))
            part = jnp.concatenate([part, part], axis=1)
            out = dot(part, held).astype(jnp.bfloat16)
            store(2 * m, p, out[:, :lanes])
            store(2 * m + 1, p, out[:, lanes:])


def unpacked(words, levels):
    re = [(word >> 16).astype(jnp.float32) * level for word, level in zip(words, levels)]
    im = [((word << 16) >> 16).astype(jnp.float32) * level for word, level in zip(words, levels)]
    return jnp.concatenate(re, axis=0), jnp.concatenate(im, axis=0)


def spread_levels(rows, scale):
    return [
        jnp.broadcast_to(jnp.exp2(row.astype(jnp.float32) * 0.25) * scale, (TILE, row.shape[1]))
        for row in rows
    ]


def spectra_kernel(stas, wins, local_wins, fused, *refs):
    parts = chunking(wins)
    chunks = len(parts)
    live_ref, pairs_ref, x_ref, table_ref, prod_ref, last_ref, level_ref, *refs = refs
    blocks, refs = refs[:chunks], refs[chunks:]
    codes, refs = refs[:chunks], refs[chunks:]
    staged, refs = refs[:chunks], refs[chunks:]
    (
        tab, raw, fold, give, got, slots_ref,
        slots_sem, tab_sem, raw_sem, fs_sem, fr_sem, ws_sem, wr_sem, send_sem, recv_sem,
    ) = refs
    sta = lax.axis_index("sta")
    win = lax.axis_index("win")
    freq = lax.axis_index("freq")
    other = 1 - freq
    samples, lanes = x_ref.shape[1:]
    windows = wins * local_wins
    sub = BAND // wins
    last = stas - 1

    def raw_copy(w):
        return pltpu.make_async_copy(x_ref.at[w], raw.at[w], raw_sem.at[w])

    side_rows = part_rows(wins)
    rows = 2 * side_rows
    reach = last - 1 if stas == 4 else 1

    def table_copy(hop, mine):
        part = lax.rem(win + hop, wins)
        at = hop * 2 + mine
        return pltpu.make_async_copy(
            table_ref.at[freq if mine else other, part], tab.at[at], tab_sem.at[at]
        )

    slots_copy = pltpu.make_async_copy(pairs_ref, slots_ref, slots_sem)
    for w in range(local_wins):
        raw_copy(w).start()
    table_copy(0, 0).start()
    slots_copy.start()

    barrier = pltpu.get_barrier_semaphore()
    pl.semaphore_signal(barrier, inc=1, device_id={"freq": other}, device_id_type=MESH)
    greeted = jnp.int32(1)
    for away in range(-reach, reach + 1):
        there = (sta + away >= 0) & (sta + away < stas)
        for hop in range(wins):
            if (away == 0) == (hop == 0):
                continue
            greeted += jnp.where(there, 1, 0)

            @pl.when(there)
            def _(away=away, hop=hop):
                to = {"sta": sta + away, "win": lax.rem(win + hop, wins)}
                pl.semaphore_signal(barrier, inc=1, device_id=to, device_id_type=MESH)

    edge = SAMPLES // 20
    span = -(-edge // 8) * 8
    begin = pl.multiple_of(freq * (samples - span), 8)
    at = begin + lax.broadcasted_iota(jnp.int32, (span, lanes), 0)
    position = jnp.where(freq == 0, at, samples - 1 - at)
    ramp = 0.5 * (1.0 - jnp.cos(math.pi * (position.astype(jnp.float32) + 0.5) / edge))
    ramp = jnp.where(position < edge, ramp, 1.0)
    sub_row = lax.broadcasted_iota(jnp.int32, (TILE, lanes), 0)
    mirror = lax.rem(TILE - sub_row, TILE)
    tiles = samples // TILE

    def mirrored(w, tile):
        value = raw[w, pl.ds(pl.multiple_of(tile * TILE, TILE), TILE), :]
        return jnp.take_along_axis(value, mirror, axis=0, mode="promise_in_bounds")

    for w in range(local_wins):
        part = slice(w * lanes, (w + 1) * lanes)
        raw_copy(w).wait()
        for hop in range(wins) if w == local_wins - 1 else []:
            for mine in range(0 if hop else 1, 2):
                table_copy(hop, mine).start()
        raw[w, pl.ds(begin, span), :] = raw[w, pl.ds(begin, span), :] * ramp

        def folding(step, before, w=w, part=part):
            for inner in range(3):
                sums, differences = [], []
                for k in range(2):
                    tile = (step * 3 + inner) * 2 + k
                    after = mirrored(w, tiles - 1 - tile)
                    back = jnp.where(sub_row == 0, before, after)
                    ahead = raw[w, pl.ds(pl.multiple_of(tile * TILE, TILE), TILE), :]
                    sums.append(ahead + back)
                    differences.append(ahead - back)
                    before = after
                at = pl.ds(pl.multiple_of((step * 3 + inner) * 2 * TILE, 2 * TILE), 2 * TILE)
                for stream, value in enumerate((sums, differences)):
                    high, low = split(jnp.concatenate(value, axis=0))
                    fold[stream, 0, at, part] = high
                    fold[stream, 1, at, part] = low
            return before

        lax.fori_loop(0, FOLD // (6 * TILE), folding, jnp.zeros((TILE, lanes), jnp.float32))

    flip = jnp.where(freq == 1, -1.0, 1.0).astype(jnp.float32)
    row = lax.broadcasted_iota(jnp.int32, (rows, 1), 0)
    signs = (jnp.where(row < side_rows, 1.0, flip), jnp.where(row < side_rows, flip, 1.0))

    count = sub // 2
    row = lax.broadcasted_iota(jnp.int32, (sub, rows), 0)
    col = lax.broadcasted_iota(jnp.int32, (sub, rows), 1)
    row = jnp.where(row < count, 2 * row, 2 * (row - count) + 1) + 2 * HALO
    col = jnp.where(col < side_rows, 2 * col, 2 * (col - side_rows) + 1)
    box = ((col - row <= HALF_WIDTH) & (row - col <= HALF_WIDTH)).astype(jnp.float32)
    box = box.astype(jnp.bfloat16)
    bin_row = lax.broadcasted_iota(jnp.int32, (sub, 1), 0)
    bin_row = jnp.where(bin_row < count, 2 * bin_row, 2 * (bin_row - count) + 1)
    station = lax.broadcasted_iota(jnp.int32, (1, local_wins * lanes), 1) % lanes
    live = (station < live_ref[0]).astype(jnp.float32)

    def partial(hop, step):
        stream = step % 2
        if stream == 0:
            table_copy(hop, step // 2).wait()
        at = hop * 2 + step // 2
        both = dot(tab[at, stream, :, :FOLD], fold[stream, 0])
        value = both[:rows] + (both[rows:] + dot(tab[at, stream, :rows, :FOLD], fold[stream, 1]))
        return value * signs[stream]

    def freq_copy(hop, step):
        return pltpu.make_async_remote_copy(
            src_ref=give.at[hop, step], dst_ref=got.at[hop, step],
            send_sem=fs_sem.at[hop, step], recv_sem=fr_sem.at[hop, step],
            device_id={"freq": other}, device_id_type=MESH,
        )

    def send_partials(hop):
        for step in range(2):
            give[hop, step] = partial(hop, step)
            if hop == 0 and step == 0:
                pl.semaphore_wait(barrier, greeted)
            freq_copy(hop, step).start()

    def encode(hop, own, slots):
        dest = lax.rem(win + hop, wins)
        for step in range(2):
            freq_copy(hop, step).wait_recv()
        summed_part = own[0] + got[hop, 0]
        differed_part = own[1] + got[hop, 1]
        real = (differed_part[:side_rows], summed_part[:side_rows])
        imag = (summed_part[side_rows:], differed_part[side_rows:])
        magnitude = jnp.concatenate([jnp.sqrt(a * a + b * b) for a, b in zip(real, imag)], axis=0)
        high, low = split(magnitude)
        summed = dot(box, high) + dot(box, low)
        bin_at = freq * BAND + dest * sub + bin_row
        counted = (
            jnp.minimum(bin_at + HALF_WIDTH, BINS - 1) - jnp.maximum(bin_at - HALF_WIDTH, 0) + 1
        ).astype(jnp.float32)
        inverse = live / jnp.maximum(summed / counted, AMP_FLOOR)
        inner = slice(HALO, HALO + count)
        white = [
            [v[parity][inner] * inverse[parity * count:(parity + 1) * count] for parity in range(2)]
            for v in (real, imag)
        ]
        for w in range(local_wins):
            part = slice(w * lanes, (w + 1) * lanes)
            values = [[v[:, part] for v in pair] for pair in white]
            peak = functools.reduce(jnp.maximum, [jnp.abs(v) for pair in values for v in pair])
            peak = jnp.max(peak, axis=0, keepdims=True)
            level = jnp.ceil(jnp.log2(jnp.maximum(peak, 1e-30)) * 4.0 + 0.01)
            factor = jnp.exp2(level * -0.25) * LEVELS
            slots[0][w:w + 1, :] = level.astype(jnp.int32)
            for c, (first, tiles) in enumerate(parts):
                base = LEVEL_ROWS if c == 0 else 0
                for parity in range(2):
                    for t in range(tiles):
                        at = slice((first + t) * TILE, (first + t + 1) * TILE)
                        top = jnp.round(values[0][parity][at] * factor).astype(jnp.int32)
                        low = jnp.round(values[1][parity][at] * factor).astype(jnp.int32)
                        to = base + ((parity * tiles + t) * local_wins + w) * TILE
                        slots[c][to:to + TILE, :] = top * 65536 + (low & 65535)

    def win_copy(c, hop):
        return pltpu.make_async_remote_copy(
            src_ref=codes[c].at[hop - 1], dst_ref=blocks[c].at[sta, win],
            send_sem=ws_sem.at[c, hop - 1], recv_sem=wr_sem.at[c, hop - 1],
            device_id={"win": lax.rem(win + hop, wins)}, device_id_type=MESH,
        )

    def slots_of(hop):
        return [blocks[c].at[sta, win] if hop == 0 else codes[c].at[hop - 1] for c in range(chunks)]

    def leave(hop):
        for c in range(chunks):
            if hop:
                win_copy(c, hop).start()
            if hop == 0 and (reach == 1 or c < 2):
                depart(c, hop)

    def picks(end, toward):
        mine = [jnp.abs(toward - slots_ref[k, end]) for k in range(2)]
        none_far, none_near = jnp.int32(-1), jnp.int32(stas)
        far = functools.reduce(jnp.maximum, [jnp.where(b < last, b, none_far) for b in mine])
        near = functools.reduce(jnp.minimum, [jnp.where(b < last, b, none_near) for b in mine])
        return jnp.clip(far, 1, last - 1), jnp.clip(near, 0, last - 2)

    slots_copy.wait()
    right_picks = picks(last, 0)
    left_picks = picks(0, last)

    def source(j):
        return lax.rem(win - j + wins, wins)

    def hop_copy(c, j, t, right, src, to, away=1):
        send, recv = (t, t if right else last - 1 - t) if reach > 1 else [t if right else last + t] * 2
        return pltpu.make_async_remote_copy(
            src_ref=src, dst_ref=blocks[c].at[to[0], to[1]],
            send_sem=send_sem.at[c, j, send], recv_sem=recv_sem.at[c, j, recv],
            device_id={"sta": sta + away if right else sta - away}, device_id_type=MESH,
        )

    def own_copy(c, j, t, right):
        to = (sta, source(j))
        return hop_copy(c, j, t, right, blocks[c].at[to[0], to[1]], to, t + 1)

    def relay_copy(c, j, t, right):
        to = (sta - t if right else sta + t, source(j))
        return hop_copy(c, j, t, right, blocks[c].at[to[0], to[1]], to)

    def whole_copy(c, j, t, right):
        return own_copy(c, j, t, right) if reach > 1 or t == 0 else relay_copy(c, j, t, right)

    def sends_whole(t, right):
        behind = sta if right else last - sta
        if reach == 1:
            return (behind >= t) & (behind < last - 1)
        return behind + t + 1 < last

    def pick_copy(c, j, right):
        to = pl.ds(last - 2, 2) if right else pl.ds(1, 2)
        send = 1 if reach > 1 else 0 if right else last
        return pltpu.make_async_remote_copy(
            src_ref=staged[c].at[:, j], dst_ref=blocks[c].at[to, source(j)],
            send_sem=send_sem.at[c, j, send], recv_sem=recv_sem.at[c, j, 0],
            device_id={"sta": sta + 1 if right else sta - 1}, device_id_type=MESH,
        )

    def arrived(c, j, t, right):
        inner = (sta >= t) & (sta < last) if right else (last - sta >= t) & (sta > 0)

        @pl.when(inner)
        def _():
            to = (sta - t if right else sta + t, source(j))
            hop_copy(c, j, t - 1, right, blocks[c].at[to[0], to[1]], to).wait_recv()

    def pick(c, j, right):
        def at(b):
            return blocks[c][b if right else last - b, source(j)]

        for which, chosen in enumerate(right_picks if right else left_picks):
            first = 1 - which
            value = at(first)
            for b in range(first + 1, first + last - 1):
                value = jnp.where(chosen == b, at(b), value)
            staged[c][1 - which if right else which, j] = value
        pick_copy(c, j, right).start()

    def depart(c, j):
        if j:
            win_copy(c, j).wait_recv()
        for k in range(reach - 1, -1, -1):
            for right in (True, False):
                @pl.when(sends_whole(k, right))
                def _(right=right, k=k):
                    own_copy(c, j, k, right).start()

    def departed(c, j):
        for k in range(reach):
            for right in (True, False):
                @pl.when(sends_whole(k, right))
                def _(right=right, k=k):
                    own_copy(c, j, k, right).wait_send()

    def event(c, j, t):
        for right in (True, False):
            behind = sta if right else last - sta
            arrived(c, j, t, right)
            if reach == 1:
                @pl.when(sends_whole(t, right))
                def _(right=right):
                    relay_copy(c, j, t, right).start()

            if t == last - 1:
                @pl.when(behind == last - 1)
                def _(right=right):
                    pick(c, j, right)

    def ended(c, j):
        for right in (True, False):
            @pl.when((sta == last) if right else (sta == 0))
            def _(right=right):
                pick_copy(c, j, right).wait_recv()

    def drain(c, j):
        for right in (True, False):
            behind = sta if right else last - sta
            for t in range(last - 1) if reach == 1 else []:
                @pl.when(sends_whole(t, right))
                def _(right=right, t=t):
                    whole_copy(c, j, t, right).wait_send()

            @pl.when(behind == last - 1)
            def _(right=right):
                pick_copy(c, j, right).wait_send()

    send_partials(0)
    own = [partial(0, step) for step in range(2, 4)]
    for hop in range(1, wins):
        send_partials(hop)
        encode(hop - 1, own, slots_of(hop - 1))
        leave(hop - 1)
        own = [partial(hop, step) for step in range(2, 4)]
    encode(wins - 1, own, slots_of(wins - 1))
    leave(wins - 1)

    def lies(b):
        at_last = jnp.where(b == last, last, jnp.where(b == right_picks[0], last - 1, last - 2))
        far = last - left_picks[0]
        at_first = jnp.where(b == 0, 0, jnp.where(b == far, 1, 2))
        return jnp.where(sta == last, at_last, jnp.where(sta == 0, at_first, b))

    left_at = lies(slots_ref[0, sta])
    right_at = lies(slots_ref[1, sta])
    order = [(s, w) for s in range(wins) for w in range(local_wins)]

    def products(c, levels, masks):
        base = LEVEL_ROWS if c == 0 else 0
        start, tiles = parts[c]
        for parity in range(2):
            for t in range(tiles):
                sides = []
                for at, level in zip((left_at, right_at), levels):
                    rows = [
                        base + ((parity * tiles + t) * local_wins + w) * TILE for _, w in order
                    ]
                    words = [blocks[c][at, s, r:r + TILE, :] for (s, _), r in zip(order, rows)]
                    sides.append(unpacked(words, level))
                first = 2 * (start + t) * TILE + parity

                def store(b, p, value, first=first):
                    prod_ref[first + 2 * b, p] = value

                pair_group(*sides, masks, store)

    def arrivals(c, part, hops):
        for t in hops:
            for j in [0] if part == 0 else range(1, wins):
                event(c, j, t)

    masks = pair_masks(windows, lanes)
    levels = []

    def finish(c):
        for j in range(wins):
            ended(c, j)
        base = LEVEL_ROWS if c == 0 else 0
        for k, at in enumerate((left_at, right_at)):
            if c == 0:
                scale = (1.0 / math.sqrt(windows) if k else 1.0) / LEVELS
                for s in range(wins):
                    level_ref[k, s] = blocks[0][at, s, :LEVEL_ROWS, :]
                rows = [blocks[0][at, s, w:w + 1, :] for s, w in order]
                levels.append(spread_levels(rows, scale))
            if c == fused:
                for s in range(wins):
                    last_ref[k, s] = blocks[c][at, s, base:, :]
        if c < fused:
            products(c, levels, masks)

    hops = range(1, last)
    if reach == 1:
        for c in range(chunks):
            for j in range(1, wins):
                depart(c, j)
        for t in hops[:-1]:
            for c in range(chunks):
                for part in range(2):
                    arrivals(c, part, [t])
        for c in range(chunks):
            for part in range(2):
                arrivals(c, part, hops[-1:])
            finish(c)
    else:
        items = [(c, part) for part in range(2) for c in range(chunks)]
        pending = list(range(chunks))
        for k, (c, part) in enumerate(items):
            for ahead, ahead_part in items[k + AHEAD:k + AHEAD + 1] if k else items[2:1 + AHEAD]:
                for j in [0] if ahead_part == 0 else range(1, wins):
                    depart(ahead, j)
            for j in [0] if part == 0 else range(1, wins):
                departed(c, j)
            arrivals(c, part, hops)
            if part and c >= chunks - 2:
                finish(pending.pop(0))
        for c in pending:
            finish(c)

    for c in range(chunks):
        for j in range(wins):
            drain(c, j)
        for hop in range(1, wins):
            win_copy(c, hop).wait_send()
    for hop in range(wins):
        for step in range(2):
            freq_copy(hop, step).wait_send()


def gathered(live, slots, x, table, fused):
    stas = lax.axis_size("sta")
    wins = lax.axis_size("win")
    local_wins, samples, lanes = x.shape
    cols = local_wins * lanes
    parts = chunking(wins)
    chunks = len(parts)
    dma = pltpu.SemaphoreType.DMA
    smem = pl.BlockSpec(memory_space=pltpu.SMEM)
    hold = pl.BlockSpec(memory_space=pltpu.HBM)
    vmem = pl.BlockSpec(memory_space=pltpu.VMEM)
    rows = [chunk_rows(c, wins, local_wins) for c in range(chunks)]
    rows_in = 2 * part_rows(wins)
    return pl.pallas_call(
        functools.partial(spectra_kernel, stas, wins, local_wins, fused),
        out_shape=(
            jax.ShapeDtypeStruct((2 * parts[fused][0] * TILE, 2, lanes, lanes), jnp.bfloat16),
            jax.ShapeDtypeStruct((2, wins, rows[fused], lanes), jnp.int32),
            jax.ShapeDtypeStruct((2, wins, LEVEL_ROWS, lanes), jnp.int32),
        ),
        in_specs=[smem, hold, hold, hold],
        out_specs=(vmem, vmem, vmem),
        scratch_shapes=[
            *[pltpu.VMEM((stas, wins, r, lanes), jnp.int32) for r in rows],
            *[pltpu.VMEM((max(1, wins - 1), r, lanes), jnp.int32) for r in rows],
            *[pltpu.VMEM((2, wins, r, lanes), jnp.int32) for r in rows],
            pltpu.VMEM((2 * wins, 2, 2 * rows_in, WIDE), jnp.bfloat16),
            pltpu.VMEM((local_wins, samples, lanes), jnp.float32),
            pltpu.VMEM((2, 2, FOLD, cols), jnp.bfloat16),
            pltpu.VMEM((wins, 2, rows_in, cols), jnp.float32),
            pltpu.VMEM((wins, 2, rows_in, cols), jnp.float32),
            pltpu.SMEM((2, stas), jnp.int32),
            dma(()), dma((2 * wins,)), dma((local_wins,)), dma((wins, 2)), dma((wins, 2)),
            dma((chunks, max(1, wins - 1))), dma((chunks, max(1, wins - 1))),
            *[dma((chunks, wins, n)) for n in ((stas - 2, stas - 1) if stas == 4 else [2 * stas - 2] * 2)],
        ],
        compiler_params=pltpu.CompilerParams(
            collective_id=0, has_side_effects=True, vmem_limit_bytes=40 << 20
        ),
        name="spectra",
    )(live, *(pltpu.with_memory_space_constraint(v, pltpu.HBM) for v in (slots, x, table)))


def finish_kernel(wins, local_wins, fused, prod_ref, last_ref, level_ref, out_ref, work, prod_sem, work_sem):
    start, tiles = chunking(wins)[fused]
    windows = wins * local_wins
    lanes = prod_ref.shape[-1]
    order = [(s, w) for s in range(wins) for w in range(local_wins)]
    shares = prod_sem.shape[0]
    share = prod_ref.shape[0] // shares

    def prod_copy(k):
        at = pl.ds(k * share, share)
        return pltpu.make_async_copy(prod_ref.at[at], out_ref.at[at], prod_sem.at[k])

    def work_copy(t):
        at = pl.ds(t * 2 * TILE, 2 * TILE)
        to = pl.ds((start + t) * 2 * TILE, 2 * TILE)
        return pltpu.make_async_copy(work.at[at], out_ref.at[to], work_sem.at[t])

    for k in range(shares):
        prod_copy(k).start()
    masks = pair_masks(windows, lanes)
    levels = [
        spread_levels(
            [level_ref[k, s, w:w + 1, :] for s, w in order],
            (1.0 / math.sqrt(windows) if k else 1.0) / LEVELS,
        )
        for k in range(2)
    ]
    for t in range(tiles):
        for parity in range(2):
            sides = []
            for k in range(2):
                rows = [((parity * tiles + t) * local_wins + w) * TILE for _, w in order]
                words = [last_ref[k, s, r:r + TILE, :] for (s, _), r in zip(order, rows)]
                sides.append(unpacked(words, levels[k]))
            first = 2 * t * TILE + parity

            def store(b, p, value, first=first):
                work[first + 2 * b, p] = value

            pair_group(*sides, masks, store)
        work_copy(t).start()
    for k in range(shares):
        prod_copy(k).wait()
    for t in range(tiles):
        work_copy(t).wait()


def finished(prod, rest, levels, fused, bins, local_wins):
    wins, lanes = rest.shape[1], rest.shape[-1]
    tiles = chunking(wins)[fused][1]
    shares = math.gcd(4, prod.shape[0])
    vmem = pl.BlockSpec(memory_space=pltpu.VMEM)
    dma = pltpu.SemaphoreType.DMA
    return pl.pallas_call(
        functools.partial(finish_kernel, wins, local_wins, fused),
        out_shape=jax.ShapeDtypeStruct((bins, 2, lanes, lanes), jnp.bfloat16),
        in_specs=[vmem, vmem, vmem],
        out_specs=pl.BlockSpec(memory_space=pltpu.HBM),
        scratch_shapes=[
            pltpu.VMEM((tiles * 2 * TILE, 2, lanes, lanes), jnp.bfloat16),
            dma((shares,)), dma((tiles,)),
        ],
        compiler_params=pltpu.CompilerParams(vmem_limit_bytes=16 << 20),
        name="finish",
    )(prod, rest, levels)


def local(table, records, valid_counts, pair_blocks):
    wins = lax.axis_size("win")
    fused = len(chunking(wins)) - 1
    x = jnp.transpose(records, (1, 2, 0))
    prod, rest, levels = gathered(valid_counts, pair_blocks.T, x, jnp.asarray(table), fused)
    return finished(prod, rest, levels, fused, BAND // wins, records.shape[1])[None, None]


def solution(mesh):
    in_specs = (P(("group", "sta"), "win", "freq"), P(("group", "sta")), P("group", None))
    out_specs = P(("group", "sta"), "freq", "win", None, None, None)
    body = functools.partial(local, dft_table(mesh.shape["win"]))
    return jax.shard_map(body, mesh=mesh, in_specs=in_specs, out_specs=out_specs, check_vma=False)
```

```python
import functools
import math

import jax
import jax.numpy as jnp
import numpy as np
from jax import lax
from jax.experimental import pallas as pl
from jax.experimental.pallas import tpu as pltpu
from jax.sharding import PartitionSpec as P

SAMPLES = 3600
BINS = 512
HALF_WIDTH = 10
AMP_FLOOR = 0.1
HALO = 8
BAND = BINS // 2
FOLD = 912
WIDE = 1024
TILE = 8
AHEAD = 3
FIRST = 4
LEVELS = 32766.0
MESH = pl.DeviceIdType.MESH


def part_rows(cuts):
    return BAND // cuts // 2 + 2 * HALO


def dft_table(cuts):
    half = SAMPLES // 2
    rows = part_rows(cuts)
    table = np.zeros((2, cuts, 2, 4 * rows, WIDE), jnp.bfloat16)
    at = np.arange(half // 2 + 1)
    weight = np.where(at == half // 2, 0.5, 1.0) / math.sqrt(SAMPLES)
    for band in range(2):
        for part in range(cuts):
            first = band * BAND + part * (BAND // cuts) - 2 * HALO
            waves = []
            for parity in range(2):
                bins = first + 2 * np.arange(rows)[:, None] + parity
                angle = (bins + 1) * at[None] % SAMPLES * (2.0 * math.pi / SAMPLES)
                inside = (bins >= 0) & (bins < BINS)
                waves.append([np.cos(angle) * inside * weight, -np.sin(angle) * inside * weight])
            summed = np.concatenate([waves[1][0], waves[0][1]])
            differed = np.concatenate([waves[0][0], waves[1][1]])
            for stream, value in enumerate((summed, differed)):
                high = value.astype(jnp.bfloat16)
                low = value - high.astype(np.float64)
                table[band, part, stream, :2 * rows, :at.size] = high
                table[band, part, stream, 2 * rows:, :at.size] = low.astype(jnp.bfloat16)
    return table


def split(value):
    high = value.astype(jnp.bfloat16)
    return high, (value - high.astype(jnp.float32)).astype(jnp.bfloat16)


def dot(a, b):
    return jnp.dot(a, b, preferred_element_type=jnp.float32)


def chunking(wins):
    tiles = BAND // wins // 2 // TILE
    counts = [tiles // 4] * 4 if tiles % 4 == 0 else [tiles - tiles // 2, tiles // 2]
    return [(sum(counts[:k]), count) for k, count in enumerate(counts)]


def pieces(wins):
    return 2 if len(chunking(wins)) == 4 else 1


def has_levels(chunk, wins):
    return chunk % (len(chunking(wins)) // pieces(wins)) == 0


def chunk_rows(chunk, wins, local_wins):
    rows = 2 * chunking(wins)[chunk][1] * TILE * local_wins
    return rows + (local_wins if has_levels(chunk, wins) else 0)


def pair_masks(windows, lanes):
    half = windows * TILE
    depth = 2 * half
    row_bin = lax.broadcasted_iota(jnp.int32, (depth, 2 * lanes), 0) % TILE
    col_odd = lax.broadcasted_iota(jnp.int32, (depth, 2 * lanes), 1) // lanes
    keep = row_bin % 2 == col_odd
    lane_pair = lax.broadcasted_iota(jnp.int32, (lanes, 2 * depth), 1) % TILE // 2
    return keep, lane_pair


def turned(value):
    high = value.astype(jnp.bfloat16).astype(jnp.float32)
    both = jnp.concatenate([high, value - high], axis=0)
    return both.T.astype(jnp.bfloat16)


def pair_group(left, right, masks, store):
    keep, lane_pair = masks
    lanes = left[0].shape[1]
    streams = (
        turned(jnp.concatenate([left[0], left[1]], axis=0)),
        turned(jnp.concatenate([left[1], -left[0]], axis=0)),
    )
    held = jnp.concatenate([right[0], right[1]], axis=0)
    held = jnp.where(keep, jnp.concatenate([held, held], axis=1), 0.0)
    high, low = split(held)
    held = jnp.concatenate([high, high, low, low], axis=0)
    for m in range(TILE // 2):
        for p in range(2):
            part = jnp.where(lane_pair == m, streams[p], jnp.zeros_like(streams[p]))
            part = jnp.concatenate([part, part], axis=1)
            out = dot(part, held).astype(jnp.bfloat16)
            store(2 * m, p, out[:, :lanes])
            store(2 * m + 1, p, out[:, lanes:])


def unpacked(words, levels):
    re = [(word >> 16).astype(jnp.float32) * level for word, level in zip(words, levels)]
    im = [((word << 16) >> 16).astype(jnp.float32) * level for word, level in zip(words, levels)]
    return jnp.concatenate(re, axis=0), jnp.concatenate(im, axis=0)


def spread_levels(rows, scale):
    return [
        jnp.broadcast_to(jnp.exp2(row.astype(jnp.float32) * 0.25) * scale, (TILE, row.shape[1]))
        for row in rows
    ]


def spectra_kernel(stas, wins, local_wins, fused, *refs):
    parts = chunking(wins)
    chunks = len(parts)
    live_ref, pairs_ref, x_ref, table_ref, prod_ref, last_ref, level_ref, *refs = refs
    blocks, refs = refs[:chunks], refs[chunks:]
    codes, refs = refs[:chunks], refs[chunks:]
    staged, refs = refs[:chunks], refs[chunks:]
    (
        tab, raw, fold, give, got, slots_ref,
        slots_sem, tab_sem, raw_sem, fs_sem, fr_sem, ws_sem, wr_sem, send_sem, recv_sem,
    ) = refs
    sta = lax.axis_index("sta")
    win = lax.axis_index("win")
    freq = lax.axis_index("freq")
    other = 1 - freq
    samples, lanes = x_ref.shape[1:]
    windows = wins * local_wins
    sub = BAND // wins
    last = stas - 1

    def raw_copy(w):
        return pltpu.make_async_copy(x_ref.at[w], raw.at[w], raw_sem.at[w])

    steps = pieces(wins)
    side_rows = part_rows(wins * steps)
    rows = 2 * side_rows
    reach = last - 1 if stas == 4 else 1

    def table_copy(piece, mine):
        part = lax.rem(win + piece // steps, wins) * steps + piece % steps
        at = piece * 2 + mine
        return pltpu.make_async_copy(
            table_ref.at[freq if mine else other, part], tab.at[at], tab_sem.at[at]
        )

    slots_copy = pltpu.make_async_copy(pairs_ref, slots_ref, slots_sem)
    for w in range(local_wins):
        raw_copy(w).start()
    table_copy(0, 0).start()
    slots_copy.start()

    barrier = pltpu.get_barrier_semaphore()
    pl.semaphore_signal(barrier, inc=1, device_id={"freq": other}, device_id_type=MESH)
    greeted = jnp.int32(1)
    for away in range(-reach, reach + 1):
        there = (sta + away >= 0) & (sta + away < stas)
        for hop in range(wins):
            if (away == 0) == (hop == 0):
                continue
            greeted += jnp.where(there, 1, 0)

            @pl.when(there)
            def _(away=away, hop=hop):
                to = {"sta": sta + away, "win": lax.rem(win + hop, wins)}
                pl.semaphore_signal(barrier, inc=1, device_id=to, device_id_type=MESH)

    edge = SAMPLES // 20
    span = -(-edge // 8) * 8
    begin = pl.multiple_of(freq * (samples - span), 8)
    at = begin + lax.broadcasted_iota(jnp.int32, (span, lanes), 0)
    position = jnp.where(freq == 0, at, samples - 1 - at)
    ramp = 0.5 * (1.0 - jnp.cos(math.pi * (position.astype(jnp.float32) + 0.5) / edge))
    ramp = jnp.where(position < edge, ramp, 1.0)
    sub_row = lax.broadcasted_iota(jnp.int32, (TILE, lanes), 0)
    mirror = lax.rem(TILE - sub_row, TILE)
    tiles = samples // TILE

    def mirrored(w, tile):
        value = raw[w, pl.ds(pl.multiple_of(tile * TILE, TILE), TILE), :]
        return jnp.take_along_axis(value, mirror, axis=0, mode="promise_in_bounds")

    for w in range(local_wins):
        part = slice(w * lanes, (w + 1) * lanes)
        raw_copy(w).wait()
        for piece in range(wins * steps) if w == local_wins - 1 else []:
            for mine in range(0 if piece else 1, 2):
                table_copy(piece, mine).start()
        raw[w, pl.ds(begin, span), :] = raw[w, pl.ds(begin, span), :] * ramp

        def folding(step, before, w=w, part=part):
            for inner in range(3):
                sums, differences = [], []
                for k in range(2):
                    tile = (step * 3 + inner) * 2 + k
                    after = mirrored(w, tiles - 1 - tile)
                    back = jnp.where(sub_row == 0, before, after)
                    ahead = raw[w, pl.ds(pl.multiple_of(tile * TILE, TILE), TILE), :]
                    sums.append(ahead + back)
                    differences.append(ahead - back)
                    before = after
                at = pl.ds(pl.multiple_of((step * 3 + inner) * 2 * TILE, 2 * TILE), 2 * TILE)
                for stream, value in enumerate((sums, differences)):
                    high, low = split(jnp.concatenate(value, axis=0))
                    fold[stream, 0, at, part] = high
                    fold[stream, 1, at, part] = low
            return before

        lax.fori_loop(0, FOLD // (6 * TILE), folding, jnp.zeros((TILE, lanes), jnp.float32))

    flip = jnp.where(freq == 1, -1.0, 1.0).astype(jnp.float32)
    row = lax.broadcasted_iota(jnp.int32, (rows, 1), 0)
    signs = (jnp.where(row < side_rows, 1.0, flip), jnp.where(row < side_rows, flip, 1.0))

    bins = sub // steps
    count = bins // 2
    row = lax.broadcasted_iota(jnp.int32, (bins, rows), 0)
    col = lax.broadcasted_iota(jnp.int32, (bins, rows), 1)
    row = jnp.where(row < count, 2 * row, 2 * (row - count) + 1) + 2 * HALO
    col = jnp.where(col < side_rows, 2 * col, 2 * (col - side_rows) + 1)
    box = ((col - row <= HALF_WIDTH) & (row - col <= HALF_WIDTH)).astype(jnp.float32)
    box = box.astype(jnp.bfloat16)
    bin_row = lax.broadcasted_iota(jnp.int32, (bins, 1), 0)
    bin_row = jnp.where(bin_row < count, 2 * bin_row, 2 * (bin_row - count) + 1)
    station = lax.broadcasted_iota(jnp.int32, (1, local_wins * lanes), 1) % lanes
    live = (station < live_ref[0]).astype(jnp.float32)

    def partial(piece, step):
        stream = step % 2
        if stream == 0:
            table_copy(piece, step // 2).wait()
        at = piece * 2 + step // 2
        both = dot(tab[at, stream, :, :FOLD], fold[stream, 0])
        value = both[:rows] + (both[rows:] + dot(tab[at, stream, :rows, :FOLD], fold[stream, 1]))
        return value * signs[stream]

    def freq_copy(piece, step):
        return pltpu.make_async_remote_copy(
            src_ref=give.at[piece, step], dst_ref=got.at[piece, step],
            send_sem=fs_sem.at[piece, step], recv_sem=fr_sem.at[piece, step],
            device_id={"freq": other}, device_id_type=MESH,
        )

    def send_partials(piece):
        for step in range(2):
            give[piece, step] = partial(piece, step)
            if piece == 0 and step == 0:
                pl.semaphore_wait(barrier, greeted)
            freq_copy(piece, step).start()

    def encode(piece, own, slots):
        dest = lax.rem(win + piece // steps, wins)
        for step in range(2):
            freq_copy(piece, step).wait_recv()
        summed_part = own[0] + got[piece, 0]
        differed_part = own[1] + got[piece, 1]
        real = (differed_part[:side_rows], summed_part[:side_rows])
        imag = (summed_part[side_rows:], differed_part[side_rows:])
        magnitude = jnp.concatenate([jnp.sqrt(a * a + b * b) for a, b in zip(real, imag)], axis=0)
        high, low = split(magnitude)
        summed = dot(box, high) + dot(box, low)
        bin_at = freq * BAND + dest * sub + piece % steps * bins + bin_row
        counted = (
            jnp.minimum(bin_at + HALF_WIDTH, BINS - 1) - jnp.maximum(bin_at - HALF_WIDTH, 0) + 1
        ).astype(jnp.float32)
        inverse = live / jnp.maximum(summed / counted, AMP_FLOOR)
        inner = slice(HALO, HALO + count)
        white = [
            [v[parity][inner] * inverse[parity * count:(parity + 1) * count] for parity in range(2)]
            for v in (real, imag)
        ]
        for w in range(local_wins):
            part = slice(w * lanes, (w + 1) * lanes)
            values = [[v[:, part] for v in pair] for pair in white]
            peak = functools.reduce(jnp.maximum, [jnp.abs(v) for pair in values for v in pair])
            peak = jnp.max(peak, axis=0, keepdims=True)
            level = jnp.ceil(jnp.log2(jnp.maximum(peak, 1e-30)) * 4.0 + 0.01)
            factor = jnp.exp2(level * -0.25) * LEVELS
            for c in range(chunks // steps * (piece % steps), chunks // steps * (piece % steps + 1)):
                first, tiles = parts[c]
                first -= piece % steps * (count // TILE)
                if has_levels(c, wins):
                    to = 2 * tiles * TILE * local_wins + w
                    slots[c][to:to + 1, :] = level.astype(jnp.int32)
                for parity in range(2):
                    for t in range(tiles):
                        at = slice((first + t) * TILE, (first + t + 1) * TILE)
                        top = jnp.round(values[0][parity][at] * factor).astype(jnp.int32)
                        low = jnp.round(values[1][parity][at] * factor).astype(jnp.int32)
                        to = ((parity * tiles + t) * local_wins + w) * TILE
                        slots[c][to:to + TILE, :] = top * 65536 + (low & 65535)

    def win_copy(c, hop):
        return pltpu.make_async_remote_copy(
            src_ref=codes[c].at[hop - 1], dst_ref=blocks[c].at[sta, win],
            send_sem=ws_sem.at[c, hop - 1], recv_sem=wr_sem.at[c, hop - 1],
            device_id={"win": lax.rem(win + hop, wins)}, device_id_type=MESH,
        )

    def slots_of(hop):
        return [blocks[c].at[sta, win] if hop == 0 else codes[c].at[hop - 1] for c in range(chunks)]

    def leave(piece):
        hop = piece // steps
        for c in range(chunks // steps * (piece % steps), chunks // steps * (piece % steps + 1)):
            if hop:
                win_copy(c, hop).start()
            elif reach == 1 or c < FIRST:
                depart(c, hop)

    def picks(end, toward):
        mine = [jnp.abs(toward - slots_ref[k, end]) for k in range(2)]
        none_far, none_near = jnp.int32(-1), jnp.int32(stas)
        far = functools.reduce(jnp.maximum, [jnp.where(b < last, b, none_far) for b in mine])
        near = functools.reduce(jnp.minimum, [jnp.where(b < last, b, none_near) for b in mine])
        return jnp.clip(far, 1, last - 1), jnp.clip(near, 0, last - 2)

    slots_copy.wait()
    right_picks = picks(last, 0)
    left_picks = picks(0, last)

    def source(j):
        return lax.rem(win - j + wins, wins)

    def hop_copy(c, j, t, right, src, to, away=1):
        send, recv = (t, t if right else last - 1 - t) if reach > 1 else [t if right else last + t] * 2
        return pltpu.make_async_remote_copy(
            src_ref=src, dst_ref=blocks[c].at[to[0], to[1]],
            send_sem=send_sem.at[c, j, send], recv_sem=recv_sem.at[c, j, recv],
            device_id={"sta": sta + away if right else sta - away}, device_id_type=MESH,
        )

    def own_copy(c, j, t, right):
        to = (sta, source(j))
        return hop_copy(c, j, t, right, blocks[c].at[to[0], to[1]], to, t + 1)

    def relay_copy(c, j, t, right):
        to = (sta - t if right else sta + t, source(j))
        return hop_copy(c, j, t, right, blocks[c].at[to[0], to[1]], to)

    def whole_copy(c, j, t, right):
        return own_copy(c, j, t, right) if reach > 1 or t == 0 else relay_copy(c, j, t, right)

    def sends_whole(t, right):
        behind = sta if right else last - sta
        if reach == 1:
            return (behind >= t) & (behind < last - 1)
        return behind + t + 1 < last

    def pick_copy(c, j, right):
        to = pl.ds(last - 2, 2) if right else pl.ds(1, 2)
        send = 1 if reach > 1 else 0 if right else last
        return pltpu.make_async_remote_copy(
            src_ref=staged[c].at[:, j], dst_ref=blocks[c].at[to, source(j)],
            send_sem=send_sem.at[c, j, send], recv_sem=recv_sem.at[c, j, 0],
            device_id={"sta": sta + 1 if right else sta - 1}, device_id_type=MESH,
        )

    def arrived(c, j, t, right):
        inner = (sta >= t) & (sta < last) if right else (last - sta >= t) & (sta > 0)

        @pl.when(inner)
        def _():
            to = (sta - t if right else sta + t, source(j))
            hop_copy(c, j, t - 1, right, blocks[c].at[to[0], to[1]], to).wait_recv()

    def pick(c, j, right):
        def at(b):
            return blocks[c][b if right else last - b, source(j)]

        for which, chosen in enumerate(right_picks if right else left_picks):
            first = 1 - which
            value = at(first)
            for b in range(first + 1, first + last - 1):
                value = jnp.where(chosen == b, at(b), value)
            staged[c][1 - which if right else which, j] = value
        pick_copy(c, j, right).start()

    def depart(c, j):
        if j:
            win_copy(c, j).wait_recv()
        for k in range(reach - 1, -1, -1):
            for right in (True, False):
                @pl.when(sends_whole(k, right))
                def _(right=right, k=k):
                    own_copy(c, j, k, right).start()

    def departed(c, j):
        for k in range(reach):
            for right in (True, False):
                @pl.when(sends_whole(k, right))
                def _(right=right, k=k):
                    own_copy(c, j, k, right).wait_send()

    def event(c, j, t):
        for right in (True, False):
            behind = sta if right else last - sta
            arrived(c, j, t, right)
            if reach == 1:
                @pl.when(sends_whole(t, right))
                def _(right=right):
                    relay_copy(c, j, t, right).start()

            if t == last - 1:
                @pl.when(behind == last - 1)
                def _(right=right):
                    pick(c, j, right)

    def ended(c, j):
        for right in (True, False):
            @pl.when((sta == last) if right else (sta == 0))
            def _(right=right):
                pick_copy(c, j, right).wait_recv()

    def drain(c, j):
        for right in (True, False):
            behind = sta if right else last - sta
            for t in range(last - 1) if reach == 1 else []:
                @pl.when(sends_whole(t, right))
                def _(right=right, t=t):
                    whole_copy(c, j, t, right).wait_send()

            @pl.when(behind == last - 1)
            def _(right=right):
                pick_copy(c, j, right).wait_send()

    send_partials(0)
    own = [partial(0, step) for step in range(2, 4)]
    for piece in range(1, wins * steps):
        send_partials(piece)
        encode(piece - 1, own, slots_of((piece - 1) // steps))
        leave(piece - 1)
        own = [partial(piece, step) for step in range(2, 4)]
    if steps > 1 and reach > 1:
        for t in range(1, last):
            event(0, 0, t)
    encode(wins * steps - 1, own, slots_of(wins - 1))
    leave(wins * steps - 1)

    def lies(b):
        at_last = jnp.where(b == last, last, jnp.where(b == right_picks[0], last - 1, last - 2))
        far = last - left_picks[0]
        at_first = jnp.where(b == 0, 0, jnp.where(b == far, 1, 2))
        return jnp.where(sta == last, at_last, jnp.where(sta == 0, at_first, b))

    left_at = lies(slots_ref[0, sta])
    right_at = lies(slots_ref[1, sta])
    order = [(s, w) for s in range(wins) for w in range(local_wins)]

    def products(c, levels, masks):
        start, tiles = parts[c]
        for parity in range(2):
            for t in range(tiles):
                sides = []
                for at, level in zip((left_at, right_at), levels):
                    rows = [((parity * tiles + t) * local_wins + w) * TILE for _, w in order]
                    words = [blocks[c][at, s, r:r + TILE, :] for (s, _), r in zip(order, rows)]
                    sides.append(unpacked(words, level))
                first = 2 * (start + t) * TILE + parity

                def store(b, p, value, first=first):
                    prod_ref[first + 2 * b, p] = value

                pair_group(*sides, masks, store)

    def arrivals(c, part, hops):
        for t in hops:
            for j in [0] if part == 0 else range(1, wins):
                event(c, j, t)

    masks = pair_masks(windows, lanes)
    levels = {}

    def finish(c):
        for j in range(wins):
            ended(c, j)
        codes_end = 2 * parts[c][1] * TILE * local_wins
        for k, at in enumerate((left_at, right_at)):
            if has_levels(c, wins):
                scale = (1.0 / math.sqrt(windows) if k else 1.0) / LEVELS
                rows = [blocks[c][at, s, codes_end + w:codes_end + w + 1, :] for s, w in order]
                levels[k] = spread_levels(rows, scale)
                for s in range(wins):
                    level_ref[k, s, :local_wins] = blocks[c][at, s, codes_end:, :]
            if c == fused:
                for s in range(wins):
                    last_ref[k, s] = blocks[c][at, s, :codes_end, :]
        if c < fused:
            products(c, (levels[0], levels[1]), masks)

    hops = range(1, last)
    if reach == 1:
        for c in range(chunks):
            for j in range(1, wins):
                depart(c, j)
        for t in hops[:-1]:
            for c in range(chunks):
                for part in range(2):
                    arrivals(c, part, [t])
        for c in range(chunks):
            for part in range(2):
                arrivals(c, part, hops[-1:])
            finish(c)
    else:
        items = [(c, part) for part in range(2) for c in range(chunks)]
        pending = list(range(chunks))
        for k, (c, part) in enumerate(items):
            for ahead, ahead_part in items[k + AHEAD:k + AHEAD + 1] if k else items[FIRST:1 + AHEAD]:
                for j in [0] if ahead_part == 0 else range(1, wins):
                    depart(ahead, j)
            for j in [0] if part == 0 else range(1, wins):
                departed(c, j)
            if k or steps == 1:
                arrivals(c, part, hops)
            if part and c >= chunks - 2:
                finish(pending.pop(0))
        for c in pending:
            finish(c)

    for c in range(chunks):
        for j in range(wins):
            drain(c, j)
        for hop in range(1, wins):
            win_copy(c, hop).wait_send()
    for piece in range(wins * steps):
        for step in range(2):
            freq_copy(piece, step).wait_send()


def gathered(live, slots, x, table, fused):
    stas = lax.axis_size("sta")
    wins = lax.axis_size("win")
    local_wins, samples, lanes = x.shape
    cols = local_wins * lanes
    parts = chunking(wins)
    chunks = len(parts)
    dma = pltpu.SemaphoreType.DMA
    smem = pl.BlockSpec(memory_space=pltpu.SMEM)
    hold = pl.BlockSpec(memory_space=pltpu.HBM)
    vmem = pl.BlockSpec(memory_space=pltpu.VMEM)
    rows = [chunk_rows(c, wins, local_wins) for c in range(chunks)]
    cuts = wins * pieces(wins)
    rows_in = 2 * part_rows(cuts)
    return pl.pallas_call(
        functools.partial(spectra_kernel, stas, wins, local_wins, fused),
        out_shape=(
            jax.ShapeDtypeStruct((2 * parts[fused][0] * TILE, 2, lanes, lanes), jnp.bfloat16),
            jax.ShapeDtypeStruct((2, wins, 2 * parts[fused][1] * TILE * local_wins, lanes), jnp.int32),
            jax.ShapeDtypeStruct((2, wins, TILE, lanes), jnp.int32),
        ),
        in_specs=[smem, hold, hold, hold],
        out_specs=(vmem, vmem, vmem),
        scratch_shapes=[
            *[pltpu.VMEM((stas, wins, r, lanes), jnp.int32) for r in rows],
            *[pltpu.VMEM((max(1, wins - 1), r, lanes), jnp.int32) for r in rows],
            *[pltpu.VMEM((2, wins, r, lanes), jnp.int32) for r in rows],
            pltpu.VMEM((2 * cuts, 2, 2 * rows_in, WIDE), jnp.bfloat16),
            pltpu.VMEM((local_wins, samples, lanes), jnp.float32),
            pltpu.VMEM((2, 2, FOLD, cols), jnp.bfloat16),
            pltpu.VMEM((cuts, 2, rows_in, cols), jnp.float32),
            pltpu.VMEM((cuts, 2, rows_in, cols), jnp.float32),
            pltpu.SMEM((2, stas), jnp.int32),
            dma(()), dma((2 * cuts,)), dma((local_wins,)), dma((cuts, 2)), dma((cuts, 2)),
            dma((chunks, max(1, wins - 1))), dma((chunks, max(1, wins - 1))),
            *[dma((chunks, wins, n)) for n in ((stas - 2, stas - 1) if stas == 4 else [2 * stas - 2] * 2)],
        ],
        compiler_params=pltpu.CompilerParams(
            collective_id=0, has_side_effects=True, vmem_limit_bytes=40 << 20
        ),
        name="spectra",
    )(live, *(pltpu.with_memory_space_constraint(v, pltpu.HBM) for v in (slots, x, table)))


def finish_kernel(wins, local_wins, fused, prod_ref, last_ref, level_ref, out_ref, work, prod_sem, work_sem):
    start, tiles = chunking(wins)[fused]
    windows = wins * local_wins
    lanes = prod_ref.shape[-1]
    order = [(s, w) for s in range(wins) for w in range(local_wins)]
    shares = prod_sem.shape[0]
    share = prod_ref.shape[0] // shares

    def prod_copy(k):
        at = pl.ds(k * share, share)
        return pltpu.make_async_copy(prod_ref.at[at], out_ref.at[at], prod_sem.at[k])

    def work_copy(t):
        at = pl.ds(t * 2 * TILE, 2 * TILE)
        to = pl.ds((start + t) * 2 * TILE, 2 * TILE)
        return pltpu.make_async_copy(work.at[at], out_ref.at[to], work_sem.at[t])

    for k in range(shares):
        prod_copy(k).start()
    masks = pair_masks(windows, lanes)
    levels = [
        spread_levels(
            [level_ref[k, s, w:w + 1, :] for s, w in order],
            (1.0 / math.sqrt(windows) if k else 1.0) / LEVELS,
        )
        for k in range(2)
    ]
    for t in range(tiles):
        for parity in range(2):
            sides = []
            for k in range(2):
                rows = [((parity * tiles + t) * local_wins + w) * TILE for _, w in order]
                words = [last_ref[k, s, r:r + TILE, :] for (s, _), r in zip(order, rows)]
                sides.append(unpacked(words, levels[k]))
            first = 2 * t * TILE + parity

            def store(b, p, value, first=first):
                work[first + 2 * b, p] = value

            pair_group(*sides, masks, store)
        work_copy(t).start()
    for k in range(shares):
        prod_copy(k).wait()
    for t in range(tiles):
        work_copy(t).wait()


def finished(prod, rest, levels, fused, bins, local_wins):
    wins, lanes = rest.shape[1], rest.shape[-1]
    tiles = chunking(wins)[fused][1]
    shares = math.gcd(4, prod.shape[0])
    vmem = pl.BlockSpec(memory_space=pltpu.VMEM)
    dma = pltpu.SemaphoreType.DMA
    return pl.pallas_call(
        functools.partial(finish_kernel, wins, local_wins, fused),
        out_shape=jax.ShapeDtypeStruct((bins, 2, lanes, lanes), jnp.bfloat16),
        in_specs=[vmem, vmem, vmem],
        out_specs=pl.BlockSpec(memory_space=pltpu.HBM),
        scratch_shapes=[
            pltpu.VMEM((tiles * 2 * TILE, 2, lanes, lanes), jnp.bfloat16),
            dma((shares,)), dma((tiles,)),
        ],
        compiler_params=pltpu.CompilerParams(vmem_limit_bytes=16 << 20),
        name="finish",
    )(prod, rest, levels)


def local(table, records, valid_counts, pair_blocks):
    wins = lax.axis_size("win")
    fused = len(chunking(wins)) - 1
    x = jnp.transpose(records, (1, 2, 0))
    prod, rest, levels = gathered(valid_counts, pair_blocks.T, x, jnp.asarray(table), fused)
    return finished(prod, rest, levels, fused, BAND // wins, records.shape[1])[None, None]


def solution(mesh):
    in_specs = (P(("group", "sta"), "win", "freq"), P(("group", "sta")), P("group", None))
    out_specs = P(("group", "sta"), "freq", "win", None, None, None)
    wins = mesh.shape["win"]
    body = functools.partial(local, dft_table(wins * pieces(wins)))
    return jax.shard_map(body, mesh=mesh, in_specs=in_specs, out_specs=out_specs, check_vma=False)
```

```python
import functools
import math

import jax
import jax.numpy as jnp
import numpy as np
from jax import lax
from jax.experimental import pallas as pl
from jax.experimental.pallas import tpu as pltpu
from jax.sharding import PartitionSpec as P

SAMPLES = 3600
BINS = 512
HALF_WIDTH = 10
AMP_FLOOR = 0.1
HALO = 8
BAND = BINS // 2
FOLD = 912
WIDE = 1024
TILE = 8
AHEAD = 3
FIRST = 4
LEVELS = 32766.0
MESH = pl.DeviceIdType.MESH


def part_rows(cuts):
    return BAND // cuts // 2 + 2 * HALO


def dft_table(cuts):
    half = SAMPLES // 2
    rows = part_rows(cuts)
    table = np.zeros((2, cuts, 2, 4 * rows, WIDE), jnp.bfloat16)
    at = np.arange(half // 2 + 1)
    weight = np.where(at == half // 2, 0.5, 1.0) / math.sqrt(SAMPLES)
    for band in range(2):
        for part in range(cuts):
            first = band * BAND + part * (BAND // cuts) - 2 * HALO
            waves = []
            for parity in range(2):
                bins = first + 2 * np.arange(rows)[:, None] + parity
                angle = (bins + 1) * at[None] % SAMPLES * (2.0 * math.pi / SAMPLES)
                inside = (bins >= 0) & (bins < BINS)
                waves.append([np.cos(angle) * inside * weight, -np.sin(angle) * inside * weight])
            summed = np.concatenate([waves[1][0], waves[0][1]])
            differed = np.concatenate([waves[0][0], waves[1][1]])
            for stream, value in enumerate((summed, differed)):
                high = value.astype(jnp.bfloat16)
                low = value - high.astype(np.float64)
                table[band, part, stream, :2 * rows, :at.size] = high
                table[band, part, stream, 2 * rows:, :at.size] = low.astype(jnp.bfloat16)
    return table


def split(value):
    high = value.astype(jnp.bfloat16)
    return high, (value - high.astype(jnp.float32)).astype(jnp.bfloat16)


def dot(a, b):
    return jnp.dot(a, b, preferred_element_type=jnp.float32)


def chunking(wins):
    tiles = BAND // wins // 2 // TILE
    counts = [tiles // 4] * 4 if tiles % 4 == 0 else [tiles - tiles // 2, tiles // 2]
    return [(sum(counts[:k]), count) for k, count in enumerate(counts)]


def pieces(wins):
    return 2 if len(chunking(wins)) == 4 else 1


def has_levels(chunk, wins):
    return chunk % (len(chunking(wins)) // pieces(wins)) == 0


def chunk_rows(chunk, wins, local_wins):
    rows = 2 * chunking(wins)[chunk][1] * TILE * local_wins
    return rows + (local_wins if has_levels(chunk, wins) else 0)


def pair_masks(windows, lanes):
    half = windows * TILE
    depth = 2 * half
    row_bin = lax.broadcasted_iota(jnp.int32, (depth, 2 * lanes), 0) % TILE
    col_odd = lax.broadcasted_iota(jnp.int32, (depth, 2 * lanes), 1) // lanes
    keep = row_bin % 2 == col_odd
    lane_pair = lax.broadcasted_iota(jnp.int32, (lanes, 2 * depth), 1) % TILE // 2
    return keep, lane_pair


def turned(value):
    high = value.astype(jnp.bfloat16).astype(jnp.float32)
    both = jnp.concatenate([high, value - high], axis=0)
    return both.T.astype(jnp.bfloat16)


def pair_group(left, right, masks, store):
    keep, lane_pair = masks
    lanes = left[0].shape[1]
    streams = (
        turned(jnp.concatenate([left[0], left[1]], axis=0)),
        turned(jnp.concatenate([left[1], -left[0]], axis=0)),
    )
    held = jnp.concatenate([right[0], right[1]], axis=0)
    held = jnp.where(keep, jnp.concatenate([held, held], axis=1), 0.0)
    high, low = split(held)
    held = jnp.concatenate([high, high, low, low], axis=0)
    for m in range(TILE // 2):
        for p in range(2):
            part = jnp.where(lane_pair == m, streams[p], jnp.zeros_like(streams[p]))
            part = jnp.concatenate([part, part], axis=1)
            out = dot(part, held).astype(jnp.bfloat16)
            store(2 * m, p, out[:, :lanes])
            store(2 * m + 1, p, out[:, lanes:])


def unpacked(words, levels):
    re = [(word >> 16).astype(jnp.float32) * level for word, level in zip(words, levels)]
    im = [((word << 16) >> 16).astype(jnp.float32) * level for word, level in zip(words, levels)]
    return jnp.concatenate(re, axis=0), jnp.concatenate(im, axis=0)


def spread_levels(rows, scale):
    return [
        jnp.broadcast_to(jnp.exp2(row.astype(jnp.float32) * 0.25) * scale, (TILE, row.shape[1]))
        for row in rows
    ]


def spectra_kernel(stas, wins, local_wins, fused, *refs):
    parts = chunking(wins)
    chunks = len(parts)
    live_ref, pairs_ref, x_ref, table_ref, prod_ref, last_ref, level_ref, *refs = refs
    blocks, refs = refs[:chunks], refs[chunks:]
    codes, refs = refs[:chunks], refs[chunks:]
    staged, refs = refs[:chunks], refs[chunks:]
    (
        tab, raw, fold, give, got, slots_ref,
        slots_sem, tab_sem, raw_sem, fs_sem, fr_sem, ws_sem, wr_sem, send_sem, recv_sem,
    ) = refs
    sta = lax.axis_index("sta")
    win = lax.axis_index("win")
    freq = lax.axis_index("freq")
    other = 1 - freq
    samples, lanes = x_ref.shape[1:]
    windows = wins * local_wins
    sub = BAND // wins
    last = stas - 1

    def raw_copy(w):
        return pltpu.make_async_copy(x_ref.at[w], raw.at[w], raw_sem.at[w])

    steps = pieces(wins)
    side_rows = part_rows(wins * steps)
    rows = 2 * side_rows
    reach = last - 1 if stas == 4 else 1

    def table_copy(piece, mine):
        part = lax.rem(win + piece // steps, wins) * steps + piece % steps
        at = piece * 2 + mine
        return pltpu.make_async_copy(
            table_ref.at[freq if mine else other, part], tab.at[at], tab_sem.at[at]
        )

    slots_copy = pltpu.make_async_copy(pairs_ref, slots_ref, slots_sem)
    for w in range(local_wins):
        raw_copy(w).start()
    table_copy(0, 0).start()
    slots_copy.start()

    barrier = pltpu.get_barrier_semaphore()
    pl.semaphore_signal(barrier, inc=1, device_id={"freq": other}, device_id_type=MESH)
    greeted = jnp.int32(1)
    for away in range(-reach, reach + 1):
        there = (sta + away >= 0) & (sta + away < stas)
        for hop in range(wins):
            if (away == 0) == (hop == 0):
                continue
            greeted += jnp.where(there, 1, 0)

            @pl.when(there)
            def _(away=away, hop=hop):
                to = {"sta": sta + away, "win": lax.rem(win + hop, wins)}
                pl.semaphore_signal(barrier, inc=1, device_id=to, device_id_type=MESH)

    edge = SAMPLES // 20
    span = -(-edge // 8) * 8
    begin = pl.multiple_of(freq * (samples - span), 8)
    at = begin + lax.broadcasted_iota(jnp.int32, (span, lanes), 0)
    position = jnp.where(freq == 0, at, samples - 1 - at)
    ramp = 0.5 * (1.0 - jnp.cos(math.pi * (position.astype(jnp.float32) + 0.5) / edge))
    ramp = jnp.where(position < edge, ramp, 1.0)
    sub_row = lax.broadcasted_iota(jnp.int32, (TILE, lanes), 0)
    mirror = lax.rem(TILE - sub_row, TILE)
    tiles = samples // TILE

    def mirrored(w, tile):
        value = raw[w, pl.ds(pl.multiple_of(tile * TILE, TILE), TILE), :]
        return jnp.take_along_axis(value, mirror, axis=0, mode="promise_in_bounds")

    for w in range(local_wins):
        part = slice(w * lanes, (w + 1) * lanes)
        raw_copy(w).wait()
        for piece in range(wins * steps) if w == local_wins - 1 else []:
            for mine in range(0 if piece else 1, 2):
                table_copy(piece, mine).start()
        raw[w, pl.ds(begin, span), :] = raw[w, pl.ds(begin, span), :] * ramp

        def folding(step, before, w=w, part=part):
            for inner in range(3):
                sums, differences = [], []
                for k in range(2):
                    tile = (step * 3 + inner) * 2 + k
                    after = mirrored(w, tiles - 1 - tile)
                    back = jnp.where(sub_row == 0, before, after)
                    ahead = raw[w, pl.ds(pl.multiple_of(tile * TILE, TILE), TILE), :]
                    sums.append(ahead + back)
                    differences.append(ahead - back)
                    before = after
                at = pl.ds(pl.multiple_of((step * 3 + inner) * 2 * TILE, 2 * TILE), 2 * TILE)
                for stream, value in enumerate((sums, differences)):
                    high, low = split(jnp.concatenate(value, axis=0))
                    fold[stream, 0, at, part] = high
                    fold[stream, 1, at, part] = low
            return before

        lax.fori_loop(0, FOLD // (6 * TILE), folding, jnp.zeros((TILE, lanes), jnp.float32))

    flip = jnp.where(freq == 1, -1.0, 1.0).astype(jnp.float32)
    row = lax.broadcasted_iota(jnp.int32, (rows, 1), 0)
    signs = (jnp.where(row < side_rows, 1.0, flip), jnp.where(row < side_rows, flip, 1.0))

    bins = sub // steps
    count = bins // 2
    row = lax.broadcasted_iota(jnp.int32, (bins, rows), 0)
    col = lax.broadcasted_iota(jnp.int32, (bins, rows), 1)
    row = jnp.where(row < count, 2 * row, 2 * (row - count) + 1) + 2 * HALO
    col = jnp.where(col < side_rows, 2 * col, 2 * (col - side_rows) + 1)
    box = ((col - row <= HALF_WIDTH) & (row - col <= HALF_WIDTH)).astype(jnp.float32)
    box = box.astype(jnp.bfloat16)
    bin_row = lax.broadcasted_iota(jnp.int32, (bins, 1), 0)
    bin_row = jnp.where(bin_row < count, 2 * bin_row, 2 * (bin_row - count) + 1)
    station = lax.broadcasted_iota(jnp.int32, (1, local_wins * lanes), 1) % lanes
    live = (station < live_ref[0]).astype(jnp.float32)

    def partial(piece, step):
        stream = step % 2
        if stream == 0:
            table_copy(piece, step // 2).wait()
        at = piece * 2 + step // 2
        both = dot(tab[at, stream, :, :FOLD], fold[stream, 0])
        value = both[:rows] + (both[rows:] + dot(tab[at, stream, :rows, :FOLD], fold[stream, 1]))
        return value * signs[stream]

    def freq_copy(piece, step):
        return pltpu.make_async_remote_copy(
            src_ref=give.at[piece, step], dst_ref=got.at[piece, step],
            send_sem=fs_sem.at[piece, step], recv_sem=fr_sem.at[piece, step],
            device_id={"freq": other}, device_id_type=MESH,
        )

    def send_partials(piece):
        for step in range(2):
            give[piece, step] = partial(piece, step)
            if piece == 0 and step == 0:
                pl.semaphore_wait(barrier, greeted)
            freq_copy(piece, step).start()

    def encode(piece, own, slots):
        dest = lax.rem(win + piece // steps, wins)
        for step in range(2):
            freq_copy(piece, step).wait_recv()
        summed_part = own[0] + got[piece, 0]
        differed_part = own[1] + got[piece, 1]
        real = (differed_part[:side_rows], summed_part[:side_rows])
        imag = (summed_part[side_rows:], differed_part[side_rows:])
        magnitude = jnp.concatenate([jnp.sqrt(a * a + b * b) for a, b in zip(real, imag)], axis=0)
        high, low = split(magnitude)
        summed = dot(box, high) + dot(box, low)
        bin_at = freq * BAND + dest * sub + piece % steps * bins + bin_row
        counted = (
            jnp.minimum(bin_at + HALF_WIDTH, BINS - 1) - jnp.maximum(bin_at - HALF_WIDTH, 0) + 1
        ).astype(jnp.float32)
        inverse = live / jnp.maximum(summed / counted, AMP_FLOOR)
        inner = slice(HALO, HALO + count)
        white = [
            [v[parity][inner] * inverse[parity * count:(parity + 1) * count] for parity in range(2)]
            for v in (real, imag)
        ]
        for w in range(local_wins):
            part = slice(w * lanes, (w + 1) * lanes)
            values = [[v[:, part] for v in pair] for pair in white]
            peak = functools.reduce(jnp.maximum, [jnp.abs(v) for pair in values for v in pair])
            peak = jnp.max(peak, axis=0, keepdims=True)
            level = jnp.ceil(jnp.log2(jnp.maximum(peak, 1e-30)) * 4.0 + 0.01)
            factor = jnp.exp2(level * -0.25) * LEVELS
            for c in range(chunks // steps * (piece % steps), chunks // steps * (piece % steps + 1)):
                first, tiles = parts[c]
                first -= piece % steps * (count // TILE)
                if has_levels(c, wins):
                    to = 2 * tiles * TILE * local_wins + w
                    slots[c][to:to + 1, :] = level.astype(jnp.int32)
                for parity in range(2):
                    for t in range(tiles):
                        at = slice((first + t) * TILE, (first + t + 1) * TILE)
                        top = jnp.round(values[0][parity][at] * factor).astype(jnp.int32)
                        low = jnp.round(values[1][parity][at] * factor).astype(jnp.int32)
                        to = ((parity * tiles + t) * local_wins + w) * TILE
                        slots[c][to:to + TILE, :] = top * 65536 + (low & 65535)

    def win_copy(c, hop):
        return pltpu.make_async_remote_copy(
            src_ref=codes[c].at[hop - 1], dst_ref=blocks[c].at[sta, win],
            send_sem=ws_sem.at[c, hop - 1], recv_sem=wr_sem.at[c, hop - 1],
            device_id={"win": lax.rem(win + hop, wins)}, device_id_type=MESH,
        )

    def slots_of(hop):
        return [blocks[c].at[sta, win] if hop == 0 else codes[c].at[hop - 1] for c in range(chunks)]

    def leave(piece):
        hop = piece // steps
        for c in range(chunks // steps * (piece % steps), chunks // steps * (piece % steps + 1)):
            if hop:
                win_copy(c, hop).start()
            elif reach == 1 or c < FIRST:
                depart(c, hop)

    def picks(end, toward):
        mine = [jnp.abs(toward - slots_ref[k, end]) for k in range(2)]
        none_far, none_near = jnp.int32(-1), jnp.int32(stas)
        far = functools.reduce(jnp.maximum, [jnp.where(b < last, b, none_far) for b in mine])
        near = functools.reduce(jnp.minimum, [jnp.where(b < last, b, none_near) for b in mine])
        return jnp.clip(far, 1, last - 1), jnp.clip(near, 0, last - 2)

    slots_copy.wait()
    right_picks = picks(last, 0)
    left_picks = picks(0, last)

    def source(j):
        return lax.rem(win - j + wins, wins)

    def hop_copy(c, j, t, right, src, to, away=1):
        send, recv = (t, t if right else last - 1 - t) if reach > 1 else [t if right else last + t] * 2
        return pltpu.make_async_remote_copy(
            src_ref=src, dst_ref=blocks[c].at[to[0], to[1]],
            send_sem=send_sem.at[c, j, send], recv_sem=recv_sem.at[c, j, recv],
            device_id={"sta": sta + away if right else sta - away}, device_id_type=MESH,
        )

    def own_copy(c, j, t, right):
        to = (sta, source(j))
        return hop_copy(c, j, t, right, blocks[c].at[to[0], to[1]], to, t + 1)

    def relay_copy(c, j, t, right):
        to = (sta - t if right else sta + t, source(j))
        return hop_copy(c, j, t, right, blocks[c].at[to[0], to[1]], to)

    def whole_copy(c, j, t, right):
        return own_copy(c, j, t, right) if reach > 1 or t == 0 else relay_copy(c, j, t, right)

    def sends_whole(t, right):
        behind = sta if right else last - sta
        if reach == 1:
            return (behind >= t) & (behind < last - 1)
        return behind + t + 1 < last

    def pick_copy(c, j, right):
        to = pl.ds(last - 2, 2) if right else pl.ds(1, 2)
        send = 1 if reach > 1 else 0 if right else last
        return pltpu.make_async_remote_copy(
            src_ref=staged[c].at[:, j], dst_ref=blocks[c].at[to, source(j)],
            send_sem=send_sem.at[c, j, send], recv_sem=recv_sem.at[c, j, 0],
            device_id={"sta": sta + 1 if right else sta - 1}, device_id_type=MESH,
        )

    def arrived(c, j, t, right):
        inner = (sta >= t) & (sta < last) if right else (last - sta >= t) & (sta > 0)

        @pl.when(inner)
        def _():
            to = (sta - t if right else sta + t, source(j))
            hop_copy(c, j, t - 1, right, blocks[c].at[to[0], to[1]], to).wait_recv()

    def pick(c, j, right):
        def at(b):
            return blocks[c][b if right else last - b, source(j)]

        for which, chosen in enumerate(right_picks if right else left_picks):
            first = 1 - which
            value = at(first)
            for b in range(first + 1, first + last - 1):
                value = jnp.where(chosen == b, at(b), value)
            staged[c][1 - which if right else which, j] = value
        pick_copy(c, j, right).start()

    def depart(c, j):
        if j:
            win_copy(c, j).wait_recv()
        for k in range(reach - 1, -1, -1):
            for right in (True, False):
                @pl.when(sends_whole(k, right))
                def _(right=right, k=k):
                    own_copy(c, j, k, right).start()

    def departed(c, j):
        for k in range(reach):
            for right in (True, False):
                @pl.when(sends_whole(k, right))
                def _(right=right, k=k):
                    own_copy(c, j, k, right).wait_send()

    def event(c, j, t):
        for right in (True, False):
            behind = sta if right else last - sta
            arrived(c, j, t, right)
            if reach == 1:
                @pl.when(sends_whole(t, right))
                def _(right=right):
                    relay_copy(c, j, t, right).start()

            if t == last - 1:
                @pl.when(behind == last - 1)
                def _(right=right):
                    pick(c, j, right)

    def ended(c, j):
        for right in (True, False):
            @pl.when((sta == last) if right else (sta == 0))
            def _(right=right):
                pick_copy(c, j, right).wait_recv()

    def drain(c, j):
        for right in (True, False):
            behind = sta if right else last - sta
            for t in range(last - 1) if reach == 1 else []:
                @pl.when(sends_whole(t, right))
                def _(right=right, t=t):
                    whole_copy(c, j, t, right).wait_send()

            @pl.when(behind == last - 1)
            def _(right=right):
                pick_copy(c, j, right).wait_send()

    send_partials(0)
    own = [partial(0, step) for step in range(2, 4)]
    for piece in range(1, wins * steps):
        send_partials(piece)
        encode(piece - 1, own, slots_of((piece - 1) // steps))
        leave(piece - 1)
        own = [partial(piece, step) for step in range(2, 4)]
    if steps > 1 and reach > 1:
        for t in range(1, last):
            event(0, 0, t)
    encode(wins * steps - 1, own, slots_of(wins - 1))
    leave(wins * steps - 1)

    def lies(b):
        at_last = jnp.where(b == last, last, jnp.where(b == right_picks[0], last - 1, last - 2))
        far = last - left_picks[0]
        at_first = jnp.where(b == 0, 0, jnp.where(b == far, 1, 2))
        return jnp.where(sta == last, at_last, jnp.where(sta == 0, at_first, b))

    left_at = lies(slots_ref[0, sta])
    right_at = lies(slots_ref[1, sta])
    order = [(s, w) for s in range(wins) for w in range(local_wins)]

    def products(c, levels, masks):
        start, tiles = parts[c]
        for parity in range(2):
            for t in range(tiles):
                sides = []
                for at, level in zip((left_at, right_at), levels):
                    rows = [((parity * tiles + t) * local_wins + w) * TILE for _, w in order]
                    words = [blocks[c][at, s, r:r + TILE, :] for (s, _), r in zip(order, rows)]
                    sides.append(unpacked(words, level))
                first = 2 * (start + t) * TILE + parity

                def store(b, p, value, first=first):
                    prod_ref[first + 2 * b, p] = value

                pair_group(*sides, masks, store)

    def arrivals(c, part, hops):
        for t in hops:
            for j in [0] if part == 0 else range(1, wins):
                event(c, j, t)

    masks = pair_masks(windows, lanes)
    levels = {}

    def finish(c):
        for j in range(wins):
            ended(c, j)
        codes_end = 2 * parts[c][1] * TILE * local_wins
        for k, at in enumerate((left_at, right_at)):
            if has_levels(c, wins):
                scale = (1.0 / math.sqrt(windows) if k else 1.0) / LEVELS
                rows = [blocks[c][at, s, codes_end + w:codes_end + w + 1, :] for s, w in order]
                levels[k] = spread_levels(rows, scale)
                for s in range(wins):
                    level_ref[k, s, :local_wins] = blocks[c][at, s, codes_end:, :]
            if c == fused:
                for s in range(wins):
                    last_ref[k, s] = blocks[c][at, s, :codes_end, :]
        if c < fused:
            products(c, (levels[0], levels[1]), masks)

    hops = range(1, last)
    if reach == 1:
        for c in range(chunks):
            for j in range(1, wins):
                depart(c, j)
        for t in hops[:-1]:
            for c in range(chunks):
                for part in range(2):
                    arrivals(c, part, [t])
        for c in range(chunks):
            for part in range(2):
                arrivals(c, part, hops[-1:])
            finish(c)
    else:
        items = [(c, part) for part in range(2) for c in range(chunks)]
        pending = list(range(chunks))
        for k, (c, part) in enumerate(items):
            leaving = [n for n in range(min(FIRST, chunks), len(items)) if max(2, n - AHEAD) == k]
            for ahead, ahead_part in [items[n] for n in leaving]:
                for j in [0] if ahead_part == 0 else range(1, wins):
                    depart(ahead, j)
            for j in [0] if part == 0 else range(1, wins):
                departed(c, j)
            if k or steps == 1:
                arrivals(c, part, hops)
            if part and c >= chunks - 2:
                finish(pending.pop(0))
        for c in pending:
            finish(c)

    for c in range(chunks):
        for j in range(wins):
            drain(c, j)
        for hop in range(1, wins):
            win_copy(c, hop).wait_send()
    for piece in range(wins * steps):
        for step in range(2):
            freq_copy(piece, step).wait_send()


def gathered(live, slots, x, table, fused):
    stas = lax.axis_size("sta")
    wins = lax.axis_size("win")
    local_wins, samples, lanes = x.shape
    cols = local_wins * lanes
    parts = chunking(wins)
    chunks = len(parts)
    dma = pltpu.SemaphoreType.DMA
    smem = pl.BlockSpec(memory_space=pltpu.SMEM)
    hold = pl.BlockSpec(memory_space=pltpu.HBM)
    vmem = pl.BlockSpec(memory_space=pltpu.VMEM)
    rows = [chunk_rows(c, wins, local_wins) for c in range(chunks)]
    cuts = wins * pieces(wins)
    rows_in = 2 * part_rows(cuts)
    return pl.pallas_call(
        functools.partial(spectra_kernel, stas, wins, local_wins, fused),
        out_shape=(
            jax.ShapeDtypeStruct((2 * parts[fused][0] * TILE, 2, lanes, lanes), jnp.bfloat16),
            jax.ShapeDtypeStruct((2, wins, 2 * parts[fused][1] * TILE * local_wins, lanes), jnp.int32),
            jax.ShapeDtypeStruct((2, wins, TILE, lanes), jnp.int32),
        ),
        in_specs=[smem, hold, hold, hold],
        out_specs=(vmem, vmem, vmem),
        scratch_shapes=[
            *[pltpu.VMEM((stas, wins, r, lanes), jnp.int32) for r in rows],
            *[pltpu.VMEM((max(1, wins - 1), r, lanes), jnp.int32) for r in rows],
            *[pltpu.VMEM((2, wins, r, lanes), jnp.int32) for r in rows],
            pltpu.VMEM((2 * cuts, 2, 2 * rows_in, WIDE), jnp.bfloat16),
            pltpu.VMEM((local_wins, samples, lanes), jnp.float32),
            pltpu.VMEM((2, 2, FOLD, cols), jnp.bfloat16),
            pltpu.VMEM((cuts, 2, rows_in, cols), jnp.float32),
            pltpu.VMEM((cuts, 2, rows_in, cols), jnp.float32),
            pltpu.SMEM((2, stas), jnp.int32),
            dma(()), dma((2 * cuts,)), dma((local_wins,)), dma((cuts, 2)), dma((cuts, 2)),
            dma((chunks, max(1, wins - 1))), dma((chunks, max(1, wins - 1))),
            *[dma((chunks, wins, n)) for n in ((stas - 2, stas - 1) if stas == 4 else [2 * stas - 2] * 2)],
        ],
        compiler_params=pltpu.CompilerParams(
            collective_id=0, has_side_effects=True, vmem_limit_bytes=40 << 20
        ),
        name="spectra",
    )(live, *(pltpu.with_memory_space_constraint(v, pltpu.HBM) for v in (slots, x, table)))


def finish_kernel(wins, local_wins, fused, prod_ref, last_ref, level_ref, out_ref, work, prod_sem, work_sem):
    start, tiles = chunking(wins)[fused]
    windows = wins * local_wins
    lanes = prod_ref.shape[-1]
    order = [(s, w) for s in range(wins) for w in range(local_wins)]
    shares = prod_sem.shape[0]
    share = prod_ref.shape[0] // shares

    def prod_copy(k):
        at = pl.ds(k * share, share)
        return pltpu.make_async_copy(prod_ref.at[at], out_ref.at[at], prod_sem.at[k])

    def work_copy(t):
        at = pl.ds(t * 2 * TILE, 2 * TILE)
        to = pl.ds((start + t) * 2 * TILE, 2 * TILE)
        return pltpu.make_async_copy(work.at[at], out_ref.at[to], work_sem.at[t])

    for k in range(shares):
        prod_copy(k).start()
    masks = pair_masks(windows, lanes)
    levels = [
        spread_levels(
            [level_ref[k, s, w:w + 1, :] for s, w in order],
            (1.0 / math.sqrt(windows) if k else 1.0) / LEVELS,
        )
        for k in range(2)
    ]
    for t in range(tiles):
        for parity in range(2):
            sides = []
            for k in range(2):
                rows = [((parity * tiles + t) * local_wins + w) * TILE for _, w in order]
                words = [last_ref[k, s, r:r + TILE, :] for (s, _), r in zip(order, rows)]
                sides.append(unpacked(words, levels[k]))
            first = 2 * t * TILE + parity

            def store(b, p, value, first=first):
                work[first + 2 * b, p] = value

            pair_group(*sides, masks, store)
        work_copy(t).start()
    for k in range(shares):
        prod_copy(k).wait()
    for t in range(tiles):
        work_copy(t).wait()


def finished(prod, rest, levels, fused, bins, local_wins):
    wins, lanes = rest.shape[1], rest.shape[-1]
    tiles = chunking(wins)[fused][1]
    shares = math.gcd(4, prod.shape[0])
    vmem = pl.BlockSpec(memory_space=pltpu.VMEM)
    dma = pltpu.SemaphoreType.DMA
    return pl.pallas_call(
        functools.partial(finish_kernel, wins, local_wins, fused),
        out_shape=jax.ShapeDtypeStruct((bins, 2, lanes, lanes), jnp.bfloat16),
        in_specs=[vmem, vmem, vmem],
        out_specs=pl.BlockSpec(memory_space=pltpu.HBM),
        scratch_shapes=[
            pltpu.VMEM((tiles * 2 * TILE, 2, lanes, lanes), jnp.bfloat16),
            dma((shares,)), dma((tiles,)),
        ],
        compiler_params=pltpu.CompilerParams(vmem_limit_bytes=16 << 20),
        name="finish",
    )(prod, rest, levels)


def local(table, records, valid_counts, pair_blocks):
    wins = lax.axis_size("win")
    fused = len(chunking(wins)) - 1
    x = jnp.transpose(records, (1, 2, 0))
    prod, rest, levels = gathered(valid_counts, pair_blocks.T, x, jnp.asarray(table), fused)
    return finished(prod, rest, levels, fused, BAND // wins, records.shape[1])[None, None]


def solution(mesh):
    in_specs = (P(("group", "sta"), "win", "freq"), P(("group", "sta")), P("group", None))
    out_specs = P(("group", "sta"), "freq", "win", None, None, None)
    wins = mesh.shape["win"]
    body = functools.partial(local, dft_table(wins * pieces(wins)))
    return jax.shard_map(body, mesh=mesh, in_specs=in_specs, out_specs=out_specs, check_vma=False)
```
